32 devices in a mesh: fsdp: 8 (over y, x, core), tensor: 4 (over z).
Axes of the slice: x: 2, y: 2, z: 4, core: 2. Of those that a mesh axis runs over, the one named last changes fastest.
Arguments:
- tokens: bfloat16 [8192, 768], P(('fsdp', 'tensor')), may hold values from -6 to 6
- ln_attn: bfloat16 [768], P('fsdp'), may hold values from 0.25 to 1.75
- ln_ff: bfloat16 [768], P('fsdp'), may hold values from 0.25 to 1.75
- ln_global: bfloat16 [768], P('fsdp'), may hold values from 0.25 to 1.75
- w_query: bfloat16 [768, 768], P('fsdp', 'tensor'), may hold values from -0.02734375 to 0.02734375
- w_key: bfloat16 [768, 768], P('fsdp', 'tensor'), may hold values from -0.21875 to 0.21875
- w_value: bfloat16 [768, 768], P('fsdp', 'tensor'), may hold values from -0.21875 to 0.21875
- w_out: bfloat16 [768, 768], P('tensor', 'fsdp'), may hold values from -1.25 to 1.25
- wi_gate: bfloat16 [768, 2048], P('fsdp', 'tensor'), may hold values from -0.21875 to 0.21875
- wi_up: bfloat16 [768, 2048], P('fsdp', 'tensor'), may hold values from -0.21875 to 0.21875
- wo_ff: bfloat16 [2048, 768], P('tensor', 'fsdp'), may hold values from -0.1875 to 0.1875
- table_local: bfloat16 [32, 12], P(None, 'tensor'), may hold values from -4 to 4
- table_global: bfloat16 [32, 12], P(None, 'tensor'), may hold values from -4 to 4
- local_onehot: int32 [128, 384, 32], replicated, may hold values from 0 to 1, as said below
- global_onehot: int32 [64, 64, 32], replicated, may hold values from 0 to 1, as said below
- segment: int32 [8, 1024], P('fsdp'), may hold values from 0 to 7, never falling along the last dimension, each value on 1 to 512 neighbouring positions
- grad_out: bfloat16 [8192, 768], P(('fsdp', 'tensor')), may hold values from -6 to 6
Outputs:
- output: bfloat16 [8192, 768], P(('fsdp', 'tensor'))
- grad_tokens: float32 [8192, 768], P(('fsdp', 'tensor'))
- grad_ln_attn: float32 [768], P('fsdp')
- grad_ln_ff: float32 [768], P('fsdp')
- grad_ln_global: float32 [768], P('fsdp')
- grad_w_query: float32 [768, 768], P('fsdp', 'tensor')
- grad_w_key: float32 [768, 768], P('fsdp', 'tensor')
- grad_w_value: float32 [768, 768], P('fsdp', 'tensor')
- grad_w_out: float32 [768, 768], P('tensor', 'fsdp')
- grad_wi_gate: float32 [768, 2048], P('fsdp', 'tensor')
- grad_wi_up: float32 [768, 2048], P('fsdp', 'tensor')
- grad_wo_ff: float32 [2048, 768], P('tensor', 'fsdp')
- grad_table_local: float32 [32, 12], P(None, 'tensor')
- grad_table_global: float32 [32, 12], P(None, 'tensor')
The draws below stay inside these ranges and needn't reach their ends.
Inputs may be any that keep to these rules, and one draw needn't show every extreme that they name: `local_onehot`: each row of the last dimension holds exactly one 1; the bucket depends only on the offset j - 128 - i. `global_onehot`: each row of the last dimension holds exactly one 1; the bucket depends only on the offset a - b. `segment`: in each sequence document numbers never fall; each of the 8 documents holds 1 to 512 positions, and one holds exactly 512.
All inputs are finite; a program needn't handle non-finite values.
Results may differ from the reference program's by a relative error of at most 0.017.
Values may be sent and summed in bfloat16 or wider, within the bound.
No kernel may reach another device: no remote copies, remote signals or barrier semaphores. Data moves between devices by JAX's collectives and lax.ppermute only.
A program may use at most 128 MiB of HBM per device.

```python
import math
import jax
import jax.numpy as jnp
import numpy as np
from jax import lax

D = 768
HEADS = 12
HEAD_DIM = 64
FF = 2048
BUCKETS = 32
INNER = 768
BLOCK = 128
GBLOCK = 16
LEN = 1024
DOCS = 8
SLOTS = 64
PIECES = 72
SEQS = 8
TOKENS = 8192


def offset_buckets(key, span_count):
    increments = jax.random.randint(key, (span_count,), 0, 2)
    return jnp.minimum(jnp.cumsum(increments, dtype=jnp.int32) - increments[0], BUCKETS // 2 - 1)


def draw_local_onehot(key, part):
    magnitude = offset_buckets(jax.random.fold_in(key, 11), 2 * BLOCK)
    rows_index = jnp.arange(BLOCK, dtype=jnp.int32)[:, None]
    cols_index = jnp.arange(3 * BLOCK, dtype=jnp.int32)[None, :]
    offset = cols_index - BLOCK - rows_index
    bucket = magnitude[jnp.abs(offset)] + jnp.where(offset > 0, BUCKETS // 2, 0)
    return (bucket[:, :, None] == jnp.arange(BUCKETS, dtype=jnp.int32)[None, None, :]).astype(jnp.int32)


def draw_global_onehot(key, part):
    magnitude = offset_buckets(jax.random.fold_in(key, 12), SLOTS)
    rows_index = jnp.arange(SLOTS, dtype=jnp.int32)[:, None]
    cols_index = jnp.arange(SLOTS, dtype=jnp.int32)[None, :]
    offset = rows_index - cols_index
    bucket = magnitude[jnp.abs(offset)] + jnp.where(offset > 0, BUCKETS // 2, 0)
    return (bucket[:, :, None] == jnp.arange(BUCKETS, dtype=jnp.int32)[None, None, :]).astype(jnp.int32)


def raised(values, key, source, target, shards_of, factor):
    owner, partner = [(jnp.arange(values.shape[position]) // (values.shape[position] // shards_of)).reshape([-1 if axis == position else 1 for axis in range(values.ndim)]) for position in (source, target)]
    chosen = jax.random.permutation(key, shards_of)[partner]
    strong = (owner == chosen) | (owner == (partner + shards_of // 2) % shards_of)
    return jnp.where(strong, factor * values, values)


def block_scale(stream_key, shape, split, low, largest):
    level = 1.0
    for dim, shards_of in split:
        heights = jax.random.uniform(jax.random.fold_in(jax.random.fold_in(stream_key, 6), dim), (shards_of,), jnp.float32, low / len(split), largest / len(split))
        level = level * jnp.repeat(jnp.exp(heights), shape[dim] // shards_of).reshape((-1,) + (1,) * (len(shape) - 1 - dim))
    return level


def split_up(amount, total, limit, skew):
    portions = [(1 << 20) // math.isqrt(standing ** skew) + 1 for standing in range(2, amount + 1)]
    rest, holding = total - limit - (amount - 1), [1] * (amount - 1)
    while rest > 0:
        candidates = [i for i in range(amount - 1) if holding[i] < limit]
        pool, remaining = sum([portions[i] for i in candidates]), rest
        for i in candidates:
            more = min(limit - holding[i], max(1, remaining * portions[i] // pool), rest)
            holding[i] = holding[i] + more
            rest = rest - more
    return np.array([limit] + holding)


def uneven_parts(rng, count, total, limit, lean):
    if count == 2:
        one = jax.random.randint(rng, (), max(1, total - limit), min(limit, total - 1) + 1)
        return jnp.stack([one, total - one])
    lengths = jnp.asarray(split_up(count, total, limit, lean), jnp.int32)
    couples = (count - 1) // 2
    giver, taker = lengths[1:1 + 2 * couples:2], lengths[2:2 + 2 * couples:2]
    room = jnp.minimum(giver - 1, limit - taker)
    passed = jax.random.randint(jax.random.fold_in(rng, 1), (couples,), 0, 1 << 20) % (room + 1)
    lengths = lengths.at[1:1 + 2 * couples:2].set(giver - passed).at[2:2 + 2 * couples:2].set(taker + passed)
    return lengths[jax.random.permutation(jax.random.fold_in(rng, 2), count)]


def scatter_about(rng, dims, spread, limit, split=(), kind=jnp.bfloat16):
    factor_of = block_scale(rng, dims, split, -0.22, 0.18) if split else 1.0
    values = jax.random.normal(rng, dims, jnp.float32) * spread * factor_of
    return jnp.minimum(jnp.maximum(values, -limit), limit).astype(kind)


def bell_draw_with(key, extent, deviation, reach, split, heavy, held_as=jnp.bfloat16):
    values = deviation * jax.random.normal(key, extent, jnp.float32)
    if split:
        values = values * block_scale(key, extent, split, -0.22, 0.18)
    return jnp.clip(raised(values, jax.random.fold_in(key, 3), *heavy), -reach, reach).astype(held_as)


def setup_inputs(seed: int = 0) -> dict:
    splits = jax.random.split(jax.random.key(seed), 18)
    return {
        "tokens": scatter_about(splits[0], (TOKENS, D), 1.0, 6.0, ((0, 32),)),
        "ln_attn": jnp.clip(1.0 + 0.15 * jax.random.normal(splits[1], (D,), jnp.float32), 0.25, 1.75).astype(jnp.bfloat16),
        "ln_ff": jnp.clip(1.0 + 0.15 * jax.random.normal(splits[2], (D,), jnp.float32), 0.25, 1.75).astype(jnp.bfloat16),
        "ln_global": jnp.clip(1.0 + 0.15 * jax.random.normal(splits[3], (D,), jnp.float32), 0.25, 1.75).astype(jnp.bfloat16),
        "w_query": scatter_about(splits[4], (D, INNER), (D * HEAD_DIM) ** -0.5, 0.02734375, ((0, 8), (1, 4))),
        "w_key": scatter_about(splits[5], (D, INNER), D ** -0.5, 0.21875, ((0, 8), (1, 4))),
        "w_value": scatter_about(splits[6], (D, INNER), D ** -0.5, 0.21875, ((0, 8), (1, 4))),
        "w_out": scatter_about(splits[7], (INNER, D), (INNER // 32) ** -0.5, 1.25, ((0, 4), (1, 8))),
        "wi_gate": scatter_about(splits[8], (D, FF), D ** -0.5, 0.21875, ((0, 8), (1, 4))),
        "wi_up": scatter_about(splits[9], (D, FF), D ** -0.5, 0.21875, ((0, 8), (1, 4))),
        "wo_ff": scatter_about(splits[10], (FF, D), (FF // 2) ** -0.5, 0.1875, ((0, 4), (1, 8))),
        "table_local": scatter_about(splits[11], (BUCKETS, HEADS), 0.7, 4.0, ((1, 4),)),
        "table_global": scatter_about(splits[12], (BUCKETS, HEADS), 0.7, 4.0, ((1, 4),)),
        "local_onehot": draw_local_onehot(jax.random.fold_in(splits[17], 71), 0),
        "global_onehot": draw_global_onehot(jax.random.fold_in(splits[17], 71), 0),
        "segment": jax.vmap(lambda own: jnp.searchsorted(jnp.cumsum(uneven_parts(own, DOCS, LEN, LEN // 2, 2)), jnp.arange(LEN), side="right"))(jax.random.split(splits[15], SEQS)).reshape((SEQS, LEN)).astype(jnp.int32),
        "grad_out": bell_draw_with(splits[16], (TOKENS, D), 1.0, 6.0, ((0, 32),), (0, 1, 32, 2.75)),
    }


tiny_eps = 1e-06
masked_score = -1e+30
highest = lax.Precision.HIGHEST

@jax.custom_vjp
def low(v):
    return lax.optimization_barrier(v.astype(jnp.bfloat16)).astype(jnp.float32)

@jax.custom_vjp
def low_back(v):
    return v

def low_keep(v):
    return (low(v), None)

def low_pass(kept, grad):
    return (grad,)

def back_keep(v):
    return (v, None)

def back_low(kept, grad):
    return (low(grad),)
low.defvjp(low_keep, low_pass)
low_back.defvjp(back_keep, back_low)

def norm_gain(values, gain):
    return values * lax.rsqrt(lax.optimization_barrier(jnp.mean(values * values, axis=-1, keepdims=True)) + tiny_eps) * gain

def key_blocks(array, fill):
    block_count = array.shape[0] // BLOCK
    edge = jnp.full((BLOCK,) + array.shape[1:], fill, array.dtype)
    padded = jnp.concatenate([edge, array, edge], axis=0)
    parts = [padded[shift * BLOCK:shift * BLOCK + array.shape[0]].reshape((block_count, BLOCK) + array.shape[1:]) for shift in range(3)]
    return jnp.concatenate(parts, axis=1)

def local_allowed(segment_row):
    block_count = segment_row.shape[0] // BLOCK
    query_seg = segment_row.reshape(block_count, BLOCK)
    key_seg = key_blocks(segment_row, -1)
    rows_index = jnp.arange(BLOCK, dtype=jnp.int32)[:, None]
    cols_index = jnp.arange(3 * BLOCK, dtype=jnp.int32)[None, :]
    within = jnp.abs(cols_index - BLOCK - rows_index) < BLOCK
    return jnp.logical_and(query_seg[:, :, None] == key_seg[:, None, :], within[None])

def layout(segment_row):
    place = jnp.arange(LEN, dtype=jnp.int32)
    before = jnp.concatenate([segment_row[:1] - 1, segment_row[:-1]])
    starts = jnp.logical_or(place % GBLOCK == 0, segment_row != before).astype(jnp.int32)
    piece = jnp.cumsum(starts, dtype=jnp.int32) - 1
    member = (piece[:, None] == jnp.arange(PIECES, dtype=jnp.int32)[None, :]).astype(jnp.float32)
    doc_hot = (segment_row[:, None] == jnp.arange(DOCS, dtype=jnp.int32)[None, :]).astype(jnp.float32)
    slot_hot = ((place // GBLOCK)[:, None] == jnp.arange(SLOTS, dtype=jnp.int32)[None, :]).astype(jnp.float32)
    piece_doc = jnp.dot(member.T, doc_hot, precision=highest)
    allowed_far = jnp.dot(doc_hot, piece_doc.T, precision=highest) > 0.5
    piece_slot = (jnp.dot(member.T, slot_hot, precision=highest) > 0.5).astype(jnp.float32)
    return (member, allowed_far, piece_slot)

def sequence_forward(tokens_row, segment_row, params, hots):
    ln_attn, ln_ff, ln_global, w_query, w_key, w_value, w_out, wi_gate, wi_up, wo_ff, table_local, table_global = params
    local_hot, global_hot = hots
    block_count = LEN // BLOCK
    member, allowed_far, piece_slot = layout(segment_row)
    normed = low(norm_gain(tokens_row, ln_attn))
    pooled = jnp.dot(member.T, normed, precision=highest)
    global_rows = low(norm_gain(pooled, ln_global))

    def project(inputs, weight):
        return low_back(low(jnp.dot(inputs, weight, precision=highest)))
    queries = project(normed, w_query).reshape(LEN, HEADS, HEAD_DIM)
    keys = project(normed, w_key).reshape(LEN, HEADS, HEAD_DIM)
    values = project(normed, w_value).reshape(LEN, HEADS, HEAD_DIM)
    far_keys = project(global_rows, w_key).reshape(PIECES, HEADS, HEAD_DIM)
    far_values = project(global_rows, w_value).reshape(PIECES, HEADS, HEAD_DIM)
    near_bias = jnp.einsum('ijn,nh->hij', local_hot, table_local, precision=highest)
    slot_bias = jnp.einsum('abn,nh->abh', global_hot, table_global, precision=highest)
    row_bias = jnp.broadcast_to(slot_bias[:, None], (SLOTS, GBLOCK, SLOTS, HEADS)).reshape(LEN, SLOTS, HEADS)
    far_bias = jnp.einsum('tgh,pg->htp', row_bias, piece_slot, precision=highest)
    query_blocks = queries.reshape(block_count, BLOCK, HEADS, HEAD_DIM)
    key_block = key_blocks(keys, 0.0)
    value_block = key_blocks(values, 0.0)
    near_scores = low_back(jnp.einsum('cihe,cjhe->hcij', query_blocks, key_block, precision=highest)) + near_bias[:, None]
    near_scores = jnp.where(local_allowed(segment_row)[None], near_scores, masked_score)
    far_scores = low_back(jnp.einsum('the,phe->htp', queries, far_keys, precision=highest)) + far_bias
    far_scores = jnp.where(allowed_far[None], far_scores, masked_score).reshape(HEADS, block_count, BLOCK, PIECES)
    scores = jnp.concatenate([near_scores, far_scores], axis=-1)
    peak = lax.optimization_barrier(jnp.max(scores, axis=-1, keepdims=True))
    expo = jnp.exp(scores - peak)
    prob = low(expo / lax.optimization_barrier(jnp.sum(expo, axis=-1, keepdims=True)))
    near_prob = prob[..., :3 * BLOCK]
    far_prob = prob[..., 3 * BLOCK:].reshape(HEADS, LEN, PIECES)
    mixed_heads = jnp.einsum('hcij,cjhe->cihe', near_prob, value_block, precision=highest).reshape(LEN, HEADS, HEAD_DIM)
    mixed_heads = mixed_heads + jnp.einsum('htp,phe->the', far_prob, far_values, precision=highest)
    attended = low_back(low(mixed_heads.reshape(LEN, INNER)))
    residual = tokens_row + low_back(jnp.dot(attended, w_out, precision=highest))
    normed_ff = low(norm_gain(residual, ln_ff))
    gate = low_back(jnp.dot(normed_ff, wi_gate, precision=highest))
    up_proj = low_back(jnp.dot(normed_ff, wi_up, precision=highest))
    hidden = low(jax.nn.gelu(gate, approximate=True) * up_proj)
    return residual + jnp.dot(hidden, wo_ff, precision=highest)

def reference(tokens, ln_attn, ln_ff, ln_global, w_query, w_key, w_value, w_out, wi_gate, wi_up, wo_ff, table_local, table_global, local_onehot, global_onehot, segment, grad_out):
    params = tuple((array_in.astype(jnp.float32) for array_in in (ln_attn, ln_ff, ln_global, w_query, w_key, w_value, w_out, wi_gate, wi_up, wo_ff, table_local, table_global)))
    hots = (local_onehot.astype(jnp.float32), global_onehot.astype(jnp.float32))
    group_size = math.gcd(SEQS, max(1, 4096 // LEN))
    group_count = SEQS // group_size
    stacked = tokens.astype(jnp.float32).reshape(group_count, group_size, LEN, D)
    seg_groups = segment.reshape(group_count, group_size, LEN)

    def forward(stacked_in, params_in):

        def one_group(pair_in):
            rows_in, segs_in = pair_in
            return jax.vmap(lambda row_one, seg_one: sequence_forward(row_one, seg_one, params_in, hots))(rows_in, segs_in)
        return lax.map(jax.checkpoint(one_group), (stacked_in, seg_groups))
    result, backward = jax.vjp(forward, stacked, params)
    grad_in, grad_params = backward(grad_out.astype(jnp.float32).reshape(result.shape))
    return (result.reshape(TOKENS, D).astype(jnp.bfloat16), grad_in.reshape(TOKENS, D), grad_params[0], grad_params[1], grad_params[2], grad_params[3], grad_params[4], grad_params[5], grad_params[6], grad_params[7], grad_params[8], grad_params[9], grad_params[10], grad_params[11])
```

```python
import jax
import jax.numpy as jnp
from jax import lax
from jax.experimental import pallas as pl
from jax.experimental.pallas import tpu as pltpu
from jax.sharding import PartitionSpec as P

D = 768
HEADS = 12
BUCKETS = 32
BLOCK = 128
GBLOCK = 16
LEN = 1024
SLOTS = 64
ROWS = 256
FAR = 32
EXT = ROWS + 2 * BLOCK
ALL = EXT + 4 * FAR
KEYS = 3 * BLOCK + 4 * FAR
HALF = D // 2
FFS = 512

f32 = jnp.float32
bf16 = jnp.bfloat16
tiny_eps = 1e-06
masked_score = -1e30
highest = lax.Precision.HIGHEST


def dot(a, b):
    return lax.dot_general(a, b, (((1,), (0,)), ((), ())), preferred_element_type=f32)


def dot_nt(a, b):
    return lax.dot_general(a, b, (((1,), (1,)), ((), ())), preferred_element_type=f32)


def dot_tn(a, b):
    return lax.dot_general(a, b, (((0,), (0,)), ((), ())), preferred_element_type=f32)


def join(w_s, own_ref, oth_ref):
    w_s[0:HALF, :] = own_ref[0]
    w_s[HALF:D, :] = oth_ref[0]


def keys_of(tile, c):
    return jnp.concatenate([tile[c * BLOCK : c * BLOCK + 3 * BLOCK], tile[EXT:ALL]], axis=0)


def attn_fwd_kernel(x_ref, own_ref, oth_ref, nb_ref, fb_ref, mask_ref, acc_ref, p_ref, r_ref, a_ref, w_s):
    join(w_s, own_ref, oth_ref)
    r = dot(x_ref[...], w_s[:, 0:640]).astype(bf16)
    r_ref[0] = r
    low = lax.broadcasted_iota(jnp.int32, (BLOCK, 128), 1) < 64
    zero = jnp.zeros((BLOCK, 128), bf16)
    for c in range(2):
        rows = slice(BLOCK + c * BLOCK, 2 * BLOCK + c * BLOCK)
        parts = []
        for j in range(3):
            tile = (lambda n: r[:, n * 128 : n * 128 + 128])
            q = tile(0)[rows] if j < 2 else tile(3)[rows]
            q = jnp.where(low, zero, q) if j == 1 else jnp.where(low, q, zero)
            k = keys_of(tile(1) if j < 2 else tile(4), c)
            v = keys_of(tile(2) if j < 2 else tile(3), c)
            bias = jnp.concatenate(
                [nb_ref[0, j], fb_ref[0, j, c * BLOCK : c * BLOCK + BLOCK]], axis=1
            ).astype(f32)
            s = dot_nt(q, k) + bias + mask_ref[c]
            e = jnp.exp(s - jnp.max(s, axis=-1, keepdims=True))
            p = (e * (1.0 / jnp.sum(e, axis=-1, keepdims=True))).astype(bf16)
            p_ref[0, c * 3 + j] = p
            parts.append(dot(p, v))
        a = jnp.concatenate(
            [jnp.where(low, 0.0, parts[2]), jnp.where(low, parts[0], parts[1])], axis=1
        ).astype(bf16)
        a_ref[0, c * BLOCK : c * BLOCK + BLOCK] = a
    part = dot_nt(a_ref[0], w_s[:, 512:768])

    @pl.when(pl.program_id(0) == 0)
    def _():
        acc_ref[...] = part

    @pl.when(pl.program_id(0) > 0)
    def _():
        acc_ref[...] += part


def slab_spec(shape):
    return pl.BlockSpec((1,) + shape, lambda i: (i,) + (0,) * len(shape))


def whole_spec(shape):
    return pl.BlockSpec(shape, lambda i: (0,) * len(shape))


def attn_fwd(x, own, oth, near_bias, far_bias, mask):
    return pl.pallas_call(
        attn_fwd_kernel,
        grid=(own.shape[0],),
        in_specs=[
            whole_spec((ALL, D)),
            slab_spec((HALF, D)),
            slab_spec((HALF, D)),
            slab_spec((3, BLOCK, 3 * BLOCK)),
            slab_spec((3, ROWS, 128)),
            whole_spec((2, BLOCK, KEYS)),
        ],
        out_specs=[
            whole_spec((ROWS, D)),
            slab_spec((6, BLOCK, KEYS)),
            slab_spec((ALL, 640)),
            slab_spec((ROWS, 256)),
        ],
        out_shape=[
            jax.ShapeDtypeStruct((ROWS, D), f32),
            jax.ShapeDtypeStruct((own.shape[0], 6, BLOCK, KEYS), bf16),
            jax.ShapeDtypeStruct((own.shape[0], ALL, 640), bf16),
            jax.ShapeDtypeStruct((own.shape[0], ROWS, 256), bf16),
        ],
        scratch_shapes=[pltpu.VMEM((D, D), bf16)],
        name="attn_fwd",
    )(x, own, oth, near_bias, far_bias, mask)


def attn_bwd_kernel(
    xt_ref, rl_ref, rlt_ref, own_ref, oth_ref, r_ref, p_ref, a_ref,
    down_ref, doth_ref, xg_ref, nbg_ref, fbg_ref, w_s, dr_s,
):
    join(w_s, own_ref, oth_ref)
    da = dot(rl_ref[...], w_s[:, 512:768]).astype(bf16)
    low = lax.broadcasted_iota(jnp.int32, (BLOCK, 128), 1) < 64
    zero = jnp.zeros((BLOCK, 128), bf16)
    r = r_ref[0]
    dr_s[...] = jnp.zeros((ALL, 640), f32)

    def add_keys(n, c, value):
        lanes = slice(n * 128, n * 128 + 128)
        dr_s[c * BLOCK : c * BLOCK + 3 * BLOCK, lanes] += value[: 3 * BLOCK]
        dr_s[EXT:ALL, lanes] += value[3 * BLOCK :]

    near = [None, None, None]
    for c in range(2):
        rows = slice(BLOCK + c * BLOCK, 2 * BLOCK + c * BLOCK)
        held = None
        for j in range(3):
            tile = (lambda n: r[:, n * 128 : n * 128 + 128])
            p = p_ref[0, c * 3 + j]
            q = tile(0)[rows] if j < 2 else tile(3)[rows]
            q = jnp.where(low, zero, q) if j == 1 else jnp.where(low, q, zero)
            k = keys_of(tile(1) if j < 2 else tile(4), c)
            v = keys_of(tile(2) if j < 2 else tile(3), c)
            do = da[c * BLOCK : c * BLOCK + BLOCK, (128 if j < 2 else 0) : (256 if j < 2 else 128)]
            do = jnp.where(low, do, zero) if j == 0 else jnp.where(low, zero, do)
            wide = p.astype(f32)
            dp = dot_nt(do, v)
            ds = wide * (dp - jnp.sum(wide * dp, axis=-1, keepdims=True))
            near[j] = ds[:, : 3 * BLOCK] if c == 0 else near[j] + ds[:, : 3 * BLOCK]
            fbg_ref[0, j, c * 8 : c * 8 + 8] = jnp.sum(
                ds[:, 3 * BLOCK :].reshape(8, GBLOCK, 128), axis=1
            )
            dl = ds.astype(bf16)
            dq = dot(dl, k)
            add_keys(1 if j < 2 else 4, c, dot_tn(dl, q))
            add_keys(2 if j < 2 else 3, c, dot_tn(p, do))
            if j == 0:
                held = dq
            elif j == 1:
                dr_s[rows, 0:128] = jnp.where(low, held, dq)
            else:
                dr_s[rows, 384:512] += jnp.where(low, dq, 0.0)
    for j in range(3):
        nbg_ref[0, j] = near[j]
    dr = dr_s[...].astype(bf16)
    part = dot_nt(dr, w_s[:, 0:640])

    @pl.when(pl.program_id(0) == 0)
    def _():
        xg_ref[...] = part

    @pl.when(pl.program_id(0) > 0)
    def _():
        xg_ref[...] += part

    for ref, base in ((down_ref, 0), (doth_ref, HALF)):
        g = dot(xt_ref[base : base + HALF, :], dr)
        go = dot(rlt_ref[base : base + HALF, :], a_ref[0])
        ref[0, :, 0:512] = g[:, 0:512].astype(bf16)
        ref[0, :, 512:640] = (g[:, 512:640] + go[:, 0:128]).astype(bf16)
        ref[0, :, 640:768] = go[:, 128:256].astype(bf16)


def attn_bwd(xt, rl, rlt, own, oth, r, p, a):
    slabs = own.shape[0]
    return pl.pallas_call(
        attn_bwd_kernel,
        grid=(slabs,),
        in_specs=[
            whole_spec((D, ALL)),
            whole_spec((ROWS, D)),
            whole_spec((D, ROWS)),
            slab_spec((HALF, D)),
            slab_spec((HALF, D)),
            slab_spec((ALL, 640)),
            slab_spec((6, BLOCK, KEYS)),
            slab_spec((ROWS, 256)),
        ],
        out_specs=[
            slab_spec((HALF, D)),
            slab_spec((HALF, D)),
            whole_spec((ALL, D)),
            slab_spec((3, BLOCK, 3 * BLOCK)),
            slab_spec((3, 16, 128)),
        ],
        out_shape=[
            jax.ShapeDtypeStruct((slabs, HALF, D), bf16),
            jax.ShapeDtypeStruct((slabs, HALF, D), bf16),
            jax.ShapeDtypeStruct((ALL, D), f32),
            jax.ShapeDtypeStruct((slabs, 3, BLOCK, 3 * BLOCK), f32),
            jax.ShapeDtypeStruct((slabs, 3, 16, 128), f32),
        ],
        scratch_shapes=[pltpu.VMEM((D, D), bf16), pltpu.VMEM((ALL, 640), f32)],
        name="attn_bwd",
    )(xt, rl, rlt, own, oth, r, p, a)


def ff_kernel(nf_ref, nft_ref, go_ref, got_ref, own_ref, oth_ref, down_ref, doth_ref, ff_ref, ng_ref, w_s):
    join(w_s, own_ref, oth_ref)
    gate = dot(nf_ref[...], w_s[:, 0:FFS])
    up = dot(nf_ref[...], w_s[:, FFS : 2 * FFS])
    hg = dot(go_ref[...], w_s[:, 2 * FFS : 3 * FFS])
    root = 0.7978845608028654
    t = jnp.tanh(root * (gate + 0.044715 * gate * gate * gate))
    cdf = 0.5 * (1.0 + t)
    act = gate * cdf
    slope = cdf + 0.5 * gate * (1.0 - t * t) * (root * (1.0 + 3.0 * 0.044715 * gate * gate))
    hidden = (act * up).astype(bf16)
    both = jnp.concatenate([(hg * up * slope).astype(bf16), (hg * act).astype(bf16)], axis=1)
    out = dot_nt(hidden, w_s[:, 2 * FFS : 3 * FFS])
    ng = dot_nt(both, w_s[:, 0 : 2 * FFS])

    @pl.when(pl.program_id(0) == 0)
    def _():
        ff_ref[...] = out
        ng_ref[...] = ng

    @pl.when(pl.program_id(0) > 0)
    def _():
        ff_ref[...] += out
        ng_ref[...] += ng

    for ref, base in ((down_ref, 0), (doth_ref, HALF)):
        ref[0, :, 0 : 2 * FFS] = dot(nft_ref[base : base + HALF, :], both).astype(bf16)
        ref[0, :, 2 * FFS : 3 * FFS] = dot(got_ref[base : base + HALF, :], hidden).astype(bf16)


def ff_both(nf, nft, go, got, own, oth):
    slabs = own.shape[0]
    return pl.pallas_call(
        ff_kernel,
        grid=(slabs,),
        in_specs=[
            whole_spec((ROWS, D)),
            whole_spec((D, ROWS)),
            whole_spec((ROWS, D)),
            whole_spec((D, ROWS)),
            slab_spec((HALF, 3 * FFS)),
            slab_spec((HALF, 3 * FFS)),
        ],
        out_specs=[
            slab_spec((HALF, 3 * FFS)),
            slab_spec((HALF, 3 * FFS)),
            whole_spec((ROWS, D)),
            whole_spec((ROWS, D)),
        ],
        out_shape=[
            jax.ShapeDtypeStruct((slabs, HALF, 3 * FFS), bf16),
            jax.ShapeDtypeStruct((slabs, HALF, 3 * FFS), bf16),
            jax.ShapeDtypeStruct((ROWS, D), f32),
            jax.ShapeDtypeStruct((ROWS, D), f32),
        ],
        scratch_shapes=[pltpu.VMEM((D, 3 * FFS), bf16)],
        name="ff_both",
    )(nf, nft, go, got, own, oth)


def swap(x, axis, mask):
    size = lax.axis_size(axis)
    return lax.ppermute(x, axis, [(i, i ^ mask) for i in range(size)])


def bit_steps(descending):
    bits = list(range(1, lax.axis_size("fsdp").bit_length() - 1))
    return bits[::-1] if descending else bits


def gather_pair(pair, descending):
    present = []
    cur = pair
    for bit in bit_steps(descending):
        place = 1 + sum(other > bit for other in present)
        cur = jnp.stack([cur, swap(cur, "fsdp", 1 << bit)], axis=place)
        present.append(bit)
    own = cur.reshape(pair.shape[0], HALF, pair.shape[-1])
    return own, swap(own, "fsdp", 1)


def gather_slabs(shard):
    others = [swap(shard, "tensor", k) for k in (1, 2, 3)]
    first = gather_pair(jnp.stack([shard, others[0]]), False)
    second = gather_pair(jnp.stack([others[1], others[2]]), True)
    return first, second


def add_wide(a, b):
    return (a.astype(f32) + b.astype(f32)).astype(a.dtype)


def scatter_pair(own, oth, descending):
    count = lax.axis_size("fsdp")
    levels = count.bit_length() - 2
    rows = own.shape[1] // (count // 2)
    cur = add_wide(own, swap(oth, "fsdp", 1))
    cur = cur.reshape((own.shape[0],) + (2,) * levels + (rows, own.shape[2]))
    left = list(range(levels, 0, -1))
    for bit in bit_steps(descending):
        place = 1 + left.index(bit)
        keep = lax.index_in_dim(cur, 0, place, keepdims=False)
        send = lax.index_in_dim(cur, 1, place, keepdims=False)
        cur = add_wide(keep, swap(send, "fsdp", 1 << bit))
        left.remove(bit)
    return cur


def scatter_tensor(slabs):
    total = slabs[0].astype(f32)
    for k in (1, 2, 3):
        total = total + swap(slabs[k], "tensor", k).astype(f32)
    return total


def rsqrt_mean(v):
    return lax.rsqrt(jnp.mean(v * v, axis=-1, keepdims=True) + tiny_eps)


def row_term(v, r, gain, e):
    eg = e * gain
    return r * eg - v * (r * r * r) * jnp.mean(eg * v, axis=-1, keepdims=True)


def hot(index, count, dtype):
    return (index[..., None] == jnp.arange(count, dtype=jnp.int32)).astype(dtype)


def per_device(
    tokens, ln_attn, ln_ff, ln_global, w_query, w_key, w_value, w_out, wi_gate, wi_up, wo_ff,
    table_local, table_global, local_onehot, global_onehot, segment, grad_out,
):
    count = lax.axis_size("fsdp")
    width = D // count
    f = lax.axis_index("fsdp")
    z = lax.axis_index("tensor")
    last = lax.axis_size("tensor") - 1

    left = lax.ppermute(tokens[ROWS - BLOCK :], "tensor", [(i, i + 1) for i in range(last)])
    right = lax.ppermute(tokens[:BLOCK], "tensor", [(i + 1, i) for i in range(last)])
    gains = jnp.stack([ln_attn, ln_ff, ln_global])[:, None, :]
    for bit in bit_steps(False) + [0]:
        gains = jnp.concatenate([gains, swap(gains, "fsdp", 1 << bit)], axis=1)
    gains = gains.reshape(3, D).astype(f32)
    gain_attn, gain_ff, gain_global = gains[0:1], gains[1:2], gains[2:3]
    tables = jnp.stack([table_local, table_global])
    tables = jnp.concatenate([tables] + [swap(tables, "tensor", k) for k in (1, 2, 3)], axis=2)

    out_t = w_out.T
    shard = jnp.concatenate(
        [
            w_query[:, :128], w_key[:, :128], w_value[:, :128], w_query[:, 128:],
            w_value[:, 128:], w_key[:, 128:], out_t[:, 128:], out_t[:, :128],
        ],
        axis=1,
    )
    attn_a, attn_b = gather_slabs(shard)
    ff_a, ff_b = gather_slabs(jnp.concatenate([wi_gate, wi_up, wo_ff.T], axis=1))

    true_at = jnp.arange(D, dtype=jnp.int32)
    place = true_at // width
    block_at = f ^ (((place & (count // 2 - 1)) << 1) | (place // (count // 2)))
    source = block_at * width + true_at % width
    order = (true_at[:, None] == source[None, :]).astype(bf16)

    ext = dot(jnp.concatenate([left, tokens, right]), order)
    go = dot(grad_out, order).astype(bf16)
    ext_r = rsqrt_mean(ext)
    normed = (ext * ext_r * gain_attn).astype(bf16)
    tok = ext[BLOCK : BLOCK + ROWS]
    tok_r = ext_r[BLOCK : BLOCK + ROWS]

    seg_row = segment[0]
    parts = seg_row.reshape(4, ROWS)
    rel = jnp.arange(4, dtype=jnp.int32) ^ z
    seg_rel = jnp.take(parts, rel, axis=0)
    here = jnp.arange(ROWS, dtype=jnp.int32)
    starts = (here % GBLOCK == 0)[None] | (
        seg_rel != jnp.concatenate([seg_rel[:, :1], seg_rel[:, :-1]], axis=1)
    )
    triangle = (here[:, None] <= here[None, :]).astype(bf16)
    piece_rel = jnp.dot(starts.astype(bf16), triangle, preferred_element_type=f32).astype(jnp.int32) - 1
    is_in = piece_rel[:, :, None] == jnp.arange(FAR, dtype=jnp.int32)
    slot_rel = rel[:, None] * (ROWS // GBLOCK) + here[None] // GBLOCK
    piece_doc = jnp.max(jnp.where(is_in, seg_rel[:, :, None], -1), axis=1).reshape(4 * FAR)
    piece_slot = jnp.max(jnp.where(is_in, slot_rel[:, :, None], -1), axis=1).reshape(4 * FAR)
    member = is_in[0].astype(bf16)
    pooled = dot_tn(member, normed[BLOCK : BLOCK + ROWS])
    pooled_r = rsqrt_mean(pooled)
    far_rows = (pooled * pooled_r * gain_global).astype(bf16)
    x = jnp.concatenate([normed, far_rows] + [swap(far_rows, "tensor", k) for k in (1, 2, 3)])

    padded = jnp.concatenate([jnp.full((BLOCK,), -1, jnp.int32), seg_row, jnp.full((BLOCK,), -1, jnp.int32)])
    seg_ext = lax.dynamic_slice(padded, (z * ROWS,), (EXT,))
    seg_own = seg_ext[BLOCK : BLOCK + ROWS].reshape(2, BLOCK)
    seg_keys = jnp.stack([seg_ext[: 3 * BLOCK], seg_ext[BLOCK:]])
    offset = jnp.arange(3 * BLOCK, dtype=jnp.int32)[None] - BLOCK - jnp.arange(BLOCK, dtype=jnp.int32)[:, None]
    near_ok = (jnp.abs(offset) < BLOCK)[None] & (seg_own[:, :, None] == seg_keys[:, None, :])
    far_ok = seg_own[:, :, None] == piece_doc[None, None, :]
    mask = jnp.where(jnp.concatenate([near_ok, far_ok], axis=2), 0.0, masked_score).astype(f32)

    offset_hot = local_onehot[0].astype(bf16)
    diagonal = lax.dot_general(
        tables[0], offset_hot, (((0,), (1,)), ((), ())), preferred_element_type=f32
    ).astype(bf16)
    wide = jnp.concatenate([diagonal, jnp.zeros((HEADS, 1), bf16)], axis=1)
    near_bias = (
        jnp.broadcast_to(wide[:, None], (HEADS, BLOCK, 3 * BLOCK + 1))
        .reshape(HEADS, -1)[:, : BLOCK * 3 * BLOCK]
        .reshape(4, 3, BLOCK, 3 * BLOCK)
    )
    own_hot = lax.dynamic_slice(global_onehot, (z * 16, 0, 0), (16, SLOTS, BUCKETS)).astype(bf16)
    slot_bias = jnp.einsum("abn,nh->hab", own_hot, tables[1], preferred_element_type=f32).astype(bf16)
    slot_hot = hot(piece_slot, SLOTS, bf16)
    far_bias = jnp.einsum("hab,pb->hap", slot_bias, slot_hot, preferred_element_type=f32).astype(bf16)
    far_bias = jnp.broadcast_to(far_bias[:, :, None], (HEADS, 16, GBLOCK, 128)).reshape(4, 3, ROWS, 128)

    acc_a, p_a, r_a, at_a = attn_fwd(x, *attn_a, near_bias[:2], far_bias[:2], mask)
    acc_b, p_b, r_b, at_b = attn_fwd(x, *attn_b, near_bias[2:], far_bias[2:], mask)
    residual = tok + (acc_a + acc_b)
    res_r = rsqrt_mean(residual)
    nf = (residual * res_r * gain_ff).astype(bf16)

    nft = nf.T
    got = go.T
    fo_a, ft_a, ffo_a, ng_a = ff_both(nf, nft, go, got, *ff_a)
    fo_b, ft_b, ffo_b, ng_b = ff_both(nf, nft, go, got, *ff_b)
    sum_fa = scatter_pair(fo_a, ft_a, False)
    sum_fb = scatter_pair(fo_b, ft_b, True)
    output = dot_nt((residual + (ffo_a + ffo_b)).astype(bf16), order).astype(bf16)
    nf_grad = ng_a + ng_b
    res_grad = go.astype(f32) + row_term(residual, res_r, gain_ff, nf_grad)
    gain_ff_grad = jnp.sum(nf_grad * residual * res_r, axis=0)
    rl = res_grad.astype(bf16)

    xt = x.T
    rlt = rl.T
    do_a, dt_a, xg_a, nb_a, fb_a = attn_bwd(xt, rl, rlt, *attn_a, r_a, p_a, at_a)
    do_b, dt_b, xg_b, nb_b, fb_b = attn_bwd(xt, rl, rlt, *attn_b, r_b, p_b, at_b)
    sum_aa = scatter_pair(do_a, dt_a, False)
    sum_ab = scatter_pair(do_b, dt_b, True)
    xg = xg_a + xg_b
    to_left = lax.ppermute(xg[:BLOCK].astype(bf16), "tensor", [(i + 1, i) for i in range(last)])
    to_right = lax.ppermute(xg[EXT - BLOCK : EXT].astype(bf16), "tensor", [(i, i + 1) for i in range(last)])
    far_grad = xg[EXT:].reshape(4, FAR, D)
    global_grad = far_grad[0]
    for k in (1, 2, 3):
        global_grad = global_grad + swap(far_grad[k].astype(bf16), "tensor", k).astype(f32)
    pooled_grad = row_term(pooled, pooled_r, gain_global, global_grad)
    gain_global_grad = jnp.sum(global_grad * pooled * pooled_r, axis=0)
    spread = jnp.dot(member.astype(f32), pooled_grad, precision=highest)
    normed_grad = (
        xg[BLOCK : BLOCK + ROWS] + jnp.concatenate([to_right, to_left]).astype(f32) + spread
    )
    grad_tokens = res_grad + row_term(tok, tok_r, gain_attn, normed_grad)
    gain_attn_grad = jnp.sum(normed_grad * tok * tok_r, axis=0)
    grad_tokens = lax.dot_general(
        grad_tokens, order.astype(f32), (((1,), (1,)), ((), ())), precision=highest
    )

    near_grad = jnp.concatenate([nb_a, nb_b]).reshape(HEADS, BLOCK * 3 * BLOCK)
    near_grad = jnp.pad(near_grad, ((0, 0), (0, BLOCK))).reshape(HEADS, BLOCK, 3 * BLOCK + 1)
    near_grad = jnp.sum(near_grad, axis=1)[:, : 3 * BLOCK]
    near_table = jnp.dot(near_grad, local_onehot[0].astype(f32), precision=highest)
    slot_grad = jnp.concatenate([fb_a, fb_b]).reshape(HEADS, 16, 128)
    slot_grad = jnp.einsum("hap,pb->hab", slot_grad, slot_hot.astype(f32), precision=highest)
    far_table = jnp.einsum("hab,abn->hn", slot_grad, own_hot.astype(f32), precision=highest)
    table_part = jnp.concatenate(
        [near_table.reshape(4, 3 * BUCKETS), far_table.reshape(4, 3 * BUCKETS)], axis=1
    )
    gain_part = jnp.stack([gain_attn_grad, gain_ff_grad, gain_global_grad])
    gain_part = gain_part.reshape(3, count, width).transpose(1, 0, 2).reshape(count, 3 * width)
    small = jnp.concatenate(
        [
            jnp.broadcast_to(gain_part[None], (4, count, 3 * width)),
            jnp.broadcast_to(table_part[:, None], (4, count, 6 * BUCKETS)),
        ],
        axis=2,
    )
    small = scatter_pair(small[:, : count // 2], small[:, count // 2 :], False)
    small = scatter_tensor(small)[0]
    gain_sum = small[: 3 * width].reshape(3, width)
    table_sum = small[3 * width :].reshape(2, 3, BUCKETS).transpose(0, 2, 1)

    ff_sum = scatter_tensor([sum_fa[0], sum_fa[1], sum_fb[0], sum_fb[1]])
    at_sum = scatter_tensor([sum_aa[0], sum_aa[1], sum_ab[0], sum_ab[1]])
    col = lambda n: at_sum[:, n * 64 : n * 64 + 64]
    grad_query = jnp.concatenate([at_sum[:, 0:128], col(6)], axis=1)
    grad_key = jnp.concatenate([at_sum[:, 128:256], col(8)], axis=1)
    grad_value = jnp.concatenate([at_sum[:, 256:384], col(7)], axis=1)
    grad_out_w = jnp.concatenate([at_sum[:, 640:768], col(9)], axis=1).T
    return (
        output,
        grad_tokens,
        gain_sum[0],
        gain_sum[1],
        gain_sum[2],
        grad_query,
        grad_key,
        grad_value,
        grad_out_w,
        ff_sum[:, 0:FFS],
        ff_sum[:, FFS : 2 * FFS],
        ff_sum[:, 2 * FFS : 3 * FFS].T,
        table_sum[0],
        table_sum[1],
    )


def solution(mesh):
    return jax.shard_map(
        per_device,
        mesh=mesh,
        in_specs=(
            P(("fsdp", "tensor"), None),
            P("fsdp"),
            P("fsdp"),
            P("fsdp"),
            P("fsdp", "tensor"),
            P("fsdp", "tensor"),
            P("fsdp", "tensor"),
            P("tensor", "fsdp"),
            P("fsdp", "tensor"),
            P("fsdp", "tensor"),
            P("tensor", "fsdp"),
            P(None, "tensor"),
            P(None, "tensor"),
            P(),
            P(),
            P("fsdp", None),
            P(("fsdp", "tensor"), None),
        ),
        out_specs=(
            P(("fsdp", "tensor"), None),
            P(("fsdp", "tensor"), None),
            P("fsdp"),
            P("fsdp"),
            P("fsdp"),
            P("fsdp", "tensor"),
            P("fsdp", "tensor"),
            P("fsdp", "tensor"),
            P("tensor", "fsdp"),
            P("fsdp", "tensor"),
            P("fsdp", "tensor"),
            P("tensor", "fsdp"),
            P(None, "tensor"),
            P(None, "tensor"),
        ),
        check_vma=False,
    )
```

```python
import jax
import jax.numpy as jnp
from jax import lax
from jax.experimental import pallas as pl
from jax.experimental.pallas import tpu as pltpu
from jax.sharding import PartitionSpec as P


D = 768
HEADS = 12
BUCKETS = 32
BLOCK = 128
GBLOCK = 16
SLOTS = 64
ROWS = 256
FAR = 32
EXT = ROWS + 2 * BLOCK
ALL = EXT + 4 * FAR
KEYS = 3 * BLOCK + 4 * FAR
HALF = D // 2
FFS = 512
WIDE = 3 * FFS + D

f32 = jnp.float32
bf16 = jnp.bfloat16
tiny_eps = 1e-06
masked_score = -1e30
highest = lax.Precision.HIGHEST


def dot(a, b):
    return lax.dot_general(a, b, (((1,), (0,)), ((), ())), preferred_element_type=f32)


def dot_nt(a, b):
    return lax.dot_general(a, b, (((1,), (1,)), ((), ())), preferred_element_type=f32)


def dot_tn(a, b):
    return lax.dot_general(a, b, (((0,), (0,)), ((), ())), preferred_element_type=f32)


def whole_spec(shape):
    return pl.BlockSpec(shape, lambda i: (0,) * len(shape))


def slab_spec(shape):
    return pl.BlockSpec((1,) + shape, lambda i: (i,) + (0,) * len(shape))


def shape_of(shape, dtype):
    return jax.ShapeDtypeStruct(shape, dtype)


def rsqrt_mean(v):
    return lax.rsqrt(jnp.mean(v * v, axis=-1, keepdims=True) + tiny_eps)


def row_term(v, r, gain, e):
    eg = e * gain
    return r * eg - v * (r * r * r) * jnp.mean(eg * v, axis=-1, keepdims=True)


def eye(rows, cols):
    at = lax.broadcasted_iota(jnp.int32, (rows, cols), 0)
    return (at == lax.broadcasted_iota(jnp.int32, (rows, cols), 1)).astype(bf16)


def pack_kernel(wq, wk, wv, wo, gate, up, down_t, out):
    rows = wq.shape[0]
    out_t = dot_nt(eye(rows, rows), wo[...]).astype(bf16)
    out[:, 0:FFS] = gate[...]
    out[:, FFS : 2 * FFS] = up[...]
    out[:, 2 * FFS : 3 * FFS] = down_t[...]
    at = 3 * FFS
    out[:, at : at + 128] = wq[:, 0:128]
    out[:, at + 128 : at + 256] = wk[:, 0:128]
    out[:, at + 256 : at + 384] = wv[:, 0:128]
    out[:, at + 384 : at + 512] = jnp.concatenate([wq[:, 128:192], wv[:, 128:192]], axis=1)
    out[:, at + 512 : at + 640] = jnp.concatenate([wk[:, 128:192], out_t[:, 128:192]], axis=1)
    out[:, at + 640 : at + 768] = out_t[:, 0:128]


def pack(*shards):
    return pl.pallas_call(
        pack_kernel, out_shape=shape_of((shards[0].shape[0], WIDE), bf16), name="pack"
    )(*shards)


def prep_kernel(left, tok, right, grad, order, gains, mem, tables, x, tokp, gop, pooled_ref, far):
    turn = order[...]
    gain = gains[0:1]
    for base, ref in ((0, left), (BLOCK, tok), (BLOCK + ROWS, right)):
        v = dot(ref[...], turn)
        x[base : base + ref.shape[0]] = (v * rsqrt_mean(v) * gain).astype(bf16)
        if ref is tok:
            tokp[...] = v.astype(bf16)
    gop[...] = dot(grad[...], turn).astype(bf16)
    pooled = dot(mem[...], x[BLOCK : BLOCK + ROWS])
    pooled_ref[...] = pooled
    rows = (pooled * rsqrt_mean(pooled) * gains[2:3]).astype(bf16)
    at = lax.broadcasted_iota(jnp.int32, rows.shape, 0)
    far[...] = jnp.where(at == FAR - 1, jnp.broadcast_to(tables[...], rows.shape), rows)


def prep(*args):
    return pl.pallas_call(
        prep_kernel,
        out_shape=[
            shape_of((EXT, D), bf16),
            shape_of((ROWS, D), bf16),
            shape_of((ROWS, D), bf16),
            shape_of((FAR, D), f32),
            shape_of((FAR, D), bf16),
        ],
        name="prep",
    )(*args)


def join(w_s, halves, step):
    for n in range(2):

        @pl.when(step == n)
        def _(n=n):
            w_s[0:HALF, :] = halves[2 * n][...]
            w_s[HALF:D, :] = halves[2 * n + 1][...]


attn_specs = [pl.BlockSpec((HALF, D), lambda i: (0, 2))] * 4
ff_specs = [pl.BlockSpec((HALF, 3 * FFS), lambda i: (0, 0))] * 4


def keys_of(tile, c):
    return jnp.concatenate([tile[c * BLOCK : c * BLOCK + 3 * BLOCK], tile[EXT:ALL]], axis=0)


def fill_x(x_s, x, fars):
    x_s[0:EXT] = x[...]
    for n, ref in enumerate(fars):
        x_s[EXT + n * FAR : EXT + n * FAR + FAR] = ref[...]


def turned(value, back):
    at = lax.broadcasted_iota(jnp.int32, value.shape, 0)
    size = value.shape[1]
    for bit in range(7):
        step = 1 << bit
        moved = pltpu.roll(value, size - step if back else step, 1)
        value = jnp.where((at >> bit) & 1 == 1, moved, value)
    return value


def attn_fwd_kernel(base, last, *refs):
    x, f0, f1, f2, f3 = refs[:5]
    halves = refs[5:9]
    near_at, far_at, tables, mask = refs[9:13]
    refs = refs[13:]
    if last:
        before, tok, gains = refs[:3]
        refs = refs[3:]
        res, nf, p_ref, r_ref, a_ref, acc, x_s, w_s = refs
    else:
        acc, p_ref, r_ref, a_ref, x_s, w_s = refs
    step = pl.program_id(0)

    @pl.when(step == 0)
    def _():
        fill_x(x_s, x, (f0, f1, f2, f3))

    join(w_s, halves, step)
    r = dot(x_s[...], w_s[:, 0:640]).astype(bf16)
    r_ref[0] = r
    low = lax.broadcasted_iota(jnp.int32, (BLOCK, 128), 1) < 64
    zero = jnp.zeros((BLOCK, 128), bf16)
    near_index = near_at[...]
    far_index = far_at[...]
    parts = [[None] * 3, [None] * 3]
    for j in range(3):
        head = (base + step) * 3 + j
        diagonal = jnp.zeros((1, 3 * BLOCK), f32)
        slots = jnp.zeros((16, 128), f32)
        for n in range(BUCKETS):
            diagonal = jnp.where(near_index == n, tables[head, n], diagonal)
            slots = jnp.where(far_index == n, tables[HEADS + head, n], slots)
        near = turned(jnp.broadcast_to(diagonal, (BLOCK, 3 * BLOCK)), False)
        q_all = r[:, 0:128] if j < 2 else r[:, 384:512]
        k_all = r[:, 128:256] if j < 2 else r[:, 512:640]
        v_all = r[:, 256:384] if j < 2 else r[:, 384:512]
        for c in range(2):
            q = q_all[BLOCK + c * BLOCK : 2 * BLOCK + c * BLOCK]
            q = jnp.where(low, zero, q) if j == 1 else jnp.where(low, q, zero)
            far = jnp.broadcast_to(slots[c * 8 : c * 8 + 8][:, None], (8, GBLOCK, 128)).reshape(BLOCK, 128)
            s = dot_nt(q, keys_of(k_all, c)) + jnp.concatenate([near, far], axis=1) + mask[c]
            e = jnp.exp(s - jnp.max(s, axis=-1, keepdims=True))
            p = (e * (1.0 / jnp.sum(e, axis=-1, keepdims=True))).astype(bf16)
            p_ref[0, c * 3 + j] = p
            parts[c][j] = dot(p, keys_of(v_all, c))
    for c in range(2):
        a_ref[0, c * BLOCK : c * BLOCK + BLOCK] = jnp.concatenate(
            [jnp.where(low, 0.0, parts[c][2]), jnp.where(low, parts[c][0], parts[c][1])], axis=1
        ).astype(bf16)
    part = dot_nt(a_ref[0], w_s[:, 512:768])

    @pl.when(step == 0)
    def _():
        acc[...] = before[...] + part if last else part

    @pl.when(step > 0)
    def _():
        acc[...] += part

    if last:

        @pl.when(step == pl.num_programs(0) - 1)
        def _():
            v = tok[...].astype(f32) + acc[...]
            res[...] = v
            nf[...] = (v * rsqrt_mean(v) * gains[1:2]).astype(bf16)


x_specs = [whole_spec((EXT, D))] + [whole_spec((FAR, D))] * 4


def attn_fwd(base, x, fars, halves, near_at, far_at, tables, mask, *rest):
    last = len(rest) > 0
    outs = [
        (slab_spec((6, BLOCK, KEYS)), shape_of((2, 6, BLOCK, KEYS), bf16)),
        (slab_spec((ALL, 640)), shape_of((2, ALL, 640), bf16)),
        (slab_spec((ROWS, 256)), shape_of((2, ROWS, 256), bf16)),
    ]
    wide = (whole_spec((ROWS, D)), shape_of((ROWS, D), f32))
    if last:
        outs = [wide, (whole_spec((ROWS, D)), shape_of((ROWS, D), bf16))] + outs
    else:
        outs = [wide] + outs
    return pl.pallas_call(
        lambda *refs: attn_fwd_kernel(base, last, *refs),
        grid=(2,),
        in_specs=x_specs
        + attn_specs
        + [
            whole_spec((1, 3 * BLOCK)),
            whole_spec((16, 128)),
            pl.BlockSpec(memory_space=pltpu.SMEM),
            whole_spec((2, BLOCK, KEYS)),
        ]
        + ([whole_spec((ROWS, D)), whole_spec((ROWS, D)), whole_spec((8, D))] if last else []),
        out_specs=[o[0] for o in outs],
        out_shape=[o[1] for o in outs],
        scratch_shapes=([pltpu.VMEM((ROWS, D), f32)] if last else [])
        + [pltpu.VMEM((ALL, D), bf16), pltpu.VMEM((D, D), bf16)],
        name="attn_fwd_b" if last else "attn_fwd_a",
    )(x, *fars, *halves, near_at, far_at, tables, mask, *rest)


def attn_bwd_kernel(last, *refs):
    x, f0, f1, f2, f3, rl = refs[:6]
    halves = refs[6:10]
    r_ref, p_ref, a_ref = refs[10:13]
    refs = refs[13:]
    if last:
        before = refs[0]
        down, doth, near_ref, far_ref, own, lo, hi, fown, s1, s2, s3, xg, x_s, w_s, dr_s = refs[1:]
    else:
        down, doth, near_ref, far_ref, xg, x_s, w_s, dr_s = refs
    step = pl.program_id(0)

    @pl.when(step == 0)
    def _():
        fill_x(x_s, x, (f0, f1, f2, f3))

    join(w_s, halves, step)
    da = dot(rl[...], w_s[:, 512:768]).astype(bf16)
    low = lax.broadcasted_iota(jnp.int32, (BLOCK, 128), 1) < 64
    zero = jnp.zeros((BLOCK, 128), bf16)
    r = r_ref[0]
    dr_s[...] = jnp.zeros((ALL, 640), f32)

    def add_keys(n, c, value):
        lanes = slice(n * 128, n * 128 + 128)
        dr_s[c * BLOCK : c * BLOCK + 3 * BLOCK, lanes] += value[: 3 * BLOCK]
        dr_s[EXT:ALL, lanes] += value[3 * BLOCK :]

    near = [None, None, None]
    for c in range(2):
        rows = slice(BLOCK + c * BLOCK, 2 * BLOCK + c * BLOCK)
        held = None
        for j in range(3):
            p = p_ref[0, c * 3 + j]
            q = r[rows, 0:128] if j < 2 else r[rows, 384:512]
            q = jnp.where(low, zero, q) if j == 1 else jnp.where(low, q, zero)
            k = keys_of(r[:, 128:256] if j < 2 else r[:, 512:640], c)
            v = keys_of(r[:, 256:384] if j < 2 else r[:, 384:512], c)
            do = da[c * BLOCK : c * BLOCK + BLOCK, (128 if j < 2 else 0) : (256 if j < 2 else 128)]
            do = jnp.where(low, do, zero) if j == 0 else jnp.where(low, zero, do)
            wide = p.astype(f32)
            dp = dot_nt(do, v)
            ds = wide * (dp - jnp.sum(wide * dp, axis=-1, keepdims=True))
            near[j] = ds[:, : 3 * BLOCK] if c == 0 else near[j] + ds[:, : 3 * BLOCK]
            far_ref[0, j, c * 8 : c * 8 + 8] = jnp.sum(
                ds[:, 3 * BLOCK :].reshape(8, GBLOCK, 128), axis=1
            )
            dl = ds.astype(bf16)
            dq = dot(dl, k)
            add_keys(1 if j < 2 else 4, c, dot_tn(dl, q))
            add_keys(2 if j < 2 else 3, c, dot_tn(p, do))
            if j == 0:
                held = dq
            elif j == 1:
                dr_s[rows, 0:128] = jnp.where(low, held, dq)
            else:
                dr_s[rows, 384:512] += jnp.where(low, dq, 0.0)
    for j in range(3):
        near_ref[0, j : j + 1] = jnp.sum(turned(near[j], True), axis=0, keepdims=True)
    dr = dr_s[...].astype(bf16)
    part = dot_nt(dr, w_s[:, 0:640])

    @pl.when(step == 0)
    def _():
        xg[...] = before[...] + part if last else part

    @pl.when(step > 0)
    def _():
        xg[...] += part

    for ref, base in ((down, 0), (doth, HALF)):
        g = dot_tn(x_s[:, base : base + HALF], dr)
        go = dot_tn(rl[:, base : base + HALF], a_ref[0])
        ref[0, :, 0:512] = g[:, 0:512].astype(bf16)
        ref[0, :, 512:640] = (g[:, 512:640] + go[:, 0:128]).astype(bf16)
        ref[0, :, 640:768] = go[:, 128:256].astype(bf16)
    if last:

        @pl.when(step == pl.num_programs(0) - 1)
        def _():
            lo[...] = xg[0:BLOCK].astype(bf16)
            own[...] = xg[BLOCK : BLOCK + ROWS]
            hi[...] = xg[BLOCK + ROWS : EXT].astype(bf16)
            fown[...] = xg[EXT : EXT + FAR]
            for n, ref in enumerate((s1, s2, s3)):
                ref[...] = xg[EXT + FAR + n * FAR : EXT + 2 * FAR + n * FAR].astype(bf16)


def attn_bwd(x, fars, rl, halves, r, p, a, *rest):
    last = len(rest) > 0
    outs = [
        (slab_spec((HALF, D)), shape_of((2, HALF, D), bf16)),
        (slab_spec((HALF, D)), shape_of((2, HALF, D), bf16)),
        (slab_spec((3, 3 * BLOCK)), shape_of((2, 3, 3 * BLOCK), f32)),
        (slab_spec((3, 16, 128)), shape_of((2, 3, 16, 128), f32)),
    ]
    if last:
        for rows, dtype in ((ROWS, f32), (BLOCK, bf16), (BLOCK, bf16), (FAR, f32)) + ((FAR, bf16),) * 3:
            outs.append((whole_spec((rows, D)), shape_of((rows, D), dtype)))
    else:
        outs.append((whole_spec((ALL, D)), shape_of((ALL, D), f32)))
    return pl.pallas_call(
        lambda *refs: attn_bwd_kernel(last, *refs),
        grid=(2,),
        in_specs=x_specs
        + [whole_spec((ROWS, D))]
        + attn_specs
        + [slab_spec((ALL, 640)), slab_spec((6, BLOCK, KEYS)), slab_spec((ROWS, 256))]
        + ([whole_spec((ALL, D))] if last else []),
        out_specs=[o[0] for o in outs],
        out_shape=[o[1] for o in outs],
        scratch_shapes=([pltpu.VMEM((ALL, D), f32)] if last else [])
        + [pltpu.VMEM((ALL, D), bf16), pltpu.VMEM((D, D), bf16), pltpu.VMEM((ALL, 640), f32)],
        name="attn_bwd_b" if last else "attn_bwd_a",
    )(x, *fars, rl, *halves, r, p, a, *rest)


def ff_kernel(last, *refs):
    nf, go = refs[:2]
    halves = refs[2:6]
    refs = refs[6:]
    if last:
        out_a, ng_a, res, gains, order = refs[:5]
        down, doth, output, res_grad, rl, gain_grad, out_acc, ng_acc, w_s = refs[5:]
    else:
        down, doth, out_acc, ng_acc, w_s = refs
    step = pl.program_id(0)
    join(w_s, halves, step)
    gate = dot(nf[...], w_s[:, 0:FFS])
    up = dot(nf[...], w_s[:, FFS : 2 * FFS])
    hg = dot(go[...], w_s[:, 2 * FFS : 3 * FFS])
    root = 0.7978845608028654
    t = jnp.tanh(root * (gate + 0.044715 * gate * gate * gate))
    cdf = 0.5 * (1.0 + t)
    act = gate * cdf
    slope = cdf + 0.5 * gate * (1.0 - t * t) * (root * (1.0 + 3.0 * 0.044715 * gate * gate))
    hidden = (act * up).astype(bf16)
    both = jnp.concatenate([(hg * up * slope).astype(bf16), (hg * act).astype(bf16)], axis=1)
    out = dot_nt(hidden, w_s[:, 2 * FFS : 3 * FFS])
    ng = dot_nt(both, w_s[:, 0 : 2 * FFS])

    @pl.when(step == 0)
    def _():
        out_acc[...] = out_a[...] + out if last else out
        ng_acc[...] = ng_a[...] + ng if last else ng

    @pl.when(step > 0)
    def _():
        out_acc[...] += out
        ng_acc[...] += ng

    for ref, base in ((down, 0), (doth, HALF)):
        ref[0, :, 0 : 2 * FFS] = dot_tn(nf[:, base : base + HALF], both).astype(bf16)
        ref[0, :, 2 * FFS : 3 * FFS] = dot_tn(go[:, base : base + HALF], hidden).astype(bf16)
    if last:

        @pl.when(step == pl.num_programs(0) - 1)
        def _():
            v = res[...]
            r = rsqrt_mean(v)
            e = ng_acc[...]
            output[...] = dot_nt((v + out_acc[...]).astype(bf16), order[...]).astype(bf16)
            total = go[...].astype(f32) + row_term(v, r, gains[1:2], e)
            res_grad[...] = total
            rl[...] = total.astype(bf16)
            gain_grad[...] = jnp.sum(e * v * r, axis=0, keepdims=True)


def ff_both(nf, go, halves, *rest):
    last = len(rest) > 0
    wide = (whole_spec((ROWS, D)), shape_of((ROWS, D), f32))
    narrow = (whole_spec((ROWS, D)), shape_of((ROWS, D), bf16))
    outs = [(slab_spec((HALF, 3 * FFS)), shape_of((2, HALF, 3 * FFS), bf16))] * 2
    if last:
        outs = outs + [narrow, wide, narrow, (whole_spec((1, D)), shape_of((1, D), f32))]
    else:
        outs = outs + [wide, wide]
    return pl.pallas_call(
        lambda *refs: ff_kernel(last, *refs),
        grid=(2,),
        in_specs=[whole_spec((ROWS, D))] * 2
        + ff_specs
        + ([whole_spec((ROWS, D))] * 3 + [whole_spec((8, D)), whole_spec((D, D))] if last else []),
        out_specs=[o[0] for o in outs],
        out_shape=[o[1] for o in outs],
        scratch_shapes=([pltpu.VMEM((ROWS, D), f32)] * 2 if last else []) + [pltpu.VMEM((D, 3 * FFS), bf16)],
        name="ff_b" if last else "ff_a",
    )(nf, go, *halves, *rest)


def post_kernel(own, lo, hi, f0, f1, f2, f3, res_grad, tok, pooled, mem, gains, order, grad, gain_grad):
    e = f0[...] + f1[...].astype(f32) + f2[...].astype(f32) + f3[...].astype(f32)
    v = pooled[...]
    r = rsqrt_mean(v)
    spread = row_term(v, r, gains[2:3], e)
    gain_grad[1:2] = jnp.sum(e * v * r, axis=0, keepdims=True)
    wide = own[...] + jnp.concatenate([lo[...], hi[...]], axis=0).astype(f32)
    for _ in range(3):
        part = spread.astype(bf16)
        wide = wide + dot_tn(mem[...], part)
        spread = spread - part.astype(f32)
    v = tok[...].astype(f32)
    r = rsqrt_mean(v)
    gain_grad[0:1] = jnp.sum(wide * v * r, axis=0, keepdims=True)
    rest = res_grad[...] + row_term(v, r, gains[0:1], wide)
    total = jnp.zeros((ROWS, D), f32)
    for _ in range(3):
        part = rest.astype(bf16)
        total = total + dot_nt(part, order[...])
        rest = rest - part.astype(f32)
    grad[...] = total


def post(*args):
    return pl.pallas_call(
        post_kernel, out_shape=[shape_of((ROWS, D), f32), shape_of((2, D), f32)], name="post"
    )(*args)


def swap(x, axis, mask):
    size = lax.axis_size(axis)
    return lax.ppermute(x, axis, [(i, i ^ mask) for i in range(size)])


def high_bits():
    return list(range(3, lax.axis_size("fsdp").bit_length() - 1))


def gather_own(slab, bits):
    first, second = bits
    one = swap(slab, "fsdp", 1 << first)
    two = swap(slab, "fsdp", 1 << second)
    both = swap(one, "fsdp", 1 << second)
    middle = [one, two] if first == 1 else [two, one]
    return jnp.concatenate([slab] + middle + [both])


def gather_high(shard):
    for bit in high_bits():
        shard = jnp.concatenate([shard, swap(shard, "fsdp", 1 << bit)], axis=0)
    return shard


def gather_tensor(x):
    got = []
    for k in (1, 2, 3):
        got.append(swap(x, "tensor", k))
    return got


def scatter_pair(own, oth, bits):
    first, second = bits
    came = swap(oth, "fsdp", 1)

    def piece(n):
        rows = slice(n * 96, n * 96 + 96)
        return own[:, rows].astype(f32) + came[:, rows].astype(f32)

    at = {1: 1, 2: 2}
    send = jnp.concatenate([piece(at[first]), piece(3)], axis=1).astype(own.dtype)
    got = swap(send, "fsdp", 1 << first)
    send = (piece(at[second]) + got[:, 96:].astype(f32)).astype(own.dtype)
    more = swap(send, "fsdp", 1 << second)
    total = (piece(0) + got[:, :96].astype(f32) + more.astype(f32)).astype(own.dtype)
    for bit in high_bits()[::-1]:
        half = total.shape[1] // 2
        total = total[:, :half] + swap(total[:, half:], "fsdp", 1 << bit)
    return total


def scatter_tensor(slabs):
    total = slabs[0].astype(f32)
    for k in (1, 2, 3):
        got = swap(slabs[k], "tensor", k)
        total = total + got.astype(f32)
    return total


def inner(
    tokens, ln_attn, ln_ff, ln_global, w_query, w_key, w_value, w_out, wi_gate, wi_up, wo_ff,
    table_local, table_global, local_onehot, global_onehot, segment, grad_out,
):
    count = lax.axis_size("fsdp")
    width = D // count
    f = lax.axis_index("fsdp")
    z = lax.axis_index("tensor")
    last = lax.axis_size("tensor") - 1
    up_one = [(i, i + 1) for i in range(last)]
    down_one = [(i + 1, i) for i in range(last)]

    gains = jnp.stack([ln_attn, ln_ff, ln_global])[:, None, :]
    for bit in high_bits() + [1, 2, 0]:
        gains = jnp.concatenate([gains, swap(gains, "fsdp", 1 << bit)], axis=1)
    gains = jnp.pad(gains.reshape(3, D).astype(f32), ((0, 5), (0, 0)))
    left = lax.ppermute(tokens[ROWS - BLOCK :], "tensor", up_one)
    right = lax.ppermute(tokens[:BLOCK], "tensor", down_one)

    shard = gather_high(pack(w_query, w_key, w_value, w_out, wi_gate, wi_up, wo_ff.T))
    slabs = [shard] + gather_tensor(shard)
    tables = jnp.concatenate([table_local.T.reshape(1, -1), table_global.T.reshape(1, -1)], axis=1)
    tables = jnp.pad(tables, ((0, 0), (0, D - tables.shape[1])))

    true_at = jnp.arange(D, dtype=jnp.int32)
    piece = true_at // 96
    high = (true_at % 96) // width
    relative = (piece // 4) | ((piece & 3) << 1) | (high << 3)
    source = (f ^ relative) * width + true_at % width
    order = (true_at[:, None] == source[None, :]).astype(bf16)

    seg_row = segment[0]
    parts = seg_row.reshape(4, ROWS)
    rel = jnp.arange(4, dtype=jnp.int32) ^ z
    seg_rel = jnp.take(parts, rel, axis=0)
    here = jnp.arange(ROWS, dtype=jnp.int32)
    starts = (here % GBLOCK == 0)[None] | (
        seg_rel != jnp.concatenate([seg_rel[:, :1], seg_rel[:, :-1]], axis=1)
    )
    triangle = (here[:, None] <= here[None, :]).astype(bf16)
    piece_rel = dot(starts.astype(bf16), triangle).astype(jnp.int32) - 1
    is_in = piece_rel[:, None, :] == jnp.arange(FAR, dtype=jnp.int32)[:, None]
    slot_rel = rel[:, None] * (ROWS // GBLOCK) + here[None] // GBLOCK
    piece_doc = jnp.max(jnp.where(is_in, seg_rel[:, None, :], -1), axis=2).reshape(4 * FAR)
    piece_slot = jnp.max(jnp.where(is_in, slot_rel[:, None, :], -1), axis=2).reshape(4 * FAR)
    member = is_in[0].astype(bf16)

    x, tok, go, pooled, far_rows = prep(left, tokens, right, grad_out, order, gains, member, tables)
    fars = [far_rows] + gather_tensor(far_rows)

    tables = jnp.stack([far[FAR - 1, : 6 * BUCKETS] for far in fars])
    tables = tables.reshape(4, 2, 3, BUCKETS).transpose(1, 0, 2, 3).reshape(2 * HEADS, BUCKETS).astype(f32)

    padded = jnp.concatenate([jnp.full((BLOCK,), -1, jnp.int32), seg_row, jnp.full((BLOCK,), -1, jnp.int32)])
    seg_ext = lax.dynamic_slice(padded, (z * ROWS,), (EXT,))
    seg_own = seg_ext[BLOCK : BLOCK + ROWS].reshape(2, BLOCK)
    seg_keys = jnp.stack([seg_ext[: 3 * BLOCK], seg_ext[BLOCK:]])
    offset = jnp.arange(3 * BLOCK, dtype=jnp.int32)[None] - BLOCK - jnp.arange(BLOCK, dtype=jnp.int32)[:, None]
    near_ok = (jnp.abs(offset) < BLOCK)[None] & (seg_own[:, :, None] == seg_keys[:, None, :])
    far_ok = seg_own[:, :, None] == piece_doc[None, None, :]
    mask = jnp.where(jnp.concatenate([near_ok, far_ok], axis=2), 0.0, masked_score).astype(f32)
    bucket = jnp.arange(BUCKETS, dtype=jnp.int32)
    near_at = jnp.sum(local_onehot[0] * bucket, axis=1)[None]
    own_hot = lax.dynamic_slice(global_onehot, (z * 16, 0, 0), (16, SLOTS, BUCKETS))
    slot_at = jnp.sum(own_hot * bucket, axis=2)
    slot_is = piece_slot[None, :] == jnp.arange(SLOTS, dtype=jnp.int32)[:, None]
    far_at = dot(slot_at.astype(bf16), slot_is.astype(bf16)).astype(jnp.int32)

    small_work = (mask, near_at, far_at, tables)
    pairs = []
    for n, slab in enumerate(slabs):
        own_half = gather_own(slab, ((1, 2), (2, 1))[n % 2])
        if n == 1:
            own_half, (mask, near_at, far_at, tables) = lax.optimization_barrier(
                (own_half, small_work)
            )
        pairs.append([own_half, swap(own_half, "fsdp", 1)])
    pair_a = pairs[0] + pairs[1]
    pair_b = pairs[2] + pairs[3]

    acc, p_a, r_a, at_a = attn_fwd(0, x, fars, pair_a, near_at, far_at, tables, mask)
    residual, nf, p_b, r_b, at_b = attn_fwd(
        2, x, fars, pair_b, near_at, far_at, tables, mask, acc, tok, gains
    )
    fo_a, ft_a, out_a, ng_a = ff_both(nf, go, pair_a)
    fo_b, ft_b, output, res_grad, rl, gain_ff_grad = ff_both(
        nf, go, pair_b, out_a, ng_a, residual, gains, order
    )
    sum_fa = scatter_pair(fo_a, ft_a, (1, 2))
    sum_fb = scatter_pair(fo_b, ft_b, (2, 1))
    do_a, dt_a, nb_a, fb_a, xg = attn_bwd(x, fars, rl, pair_a, r_a, p_a, at_a)
    do_b, dt_b, nb_b, fb_b, own, lo, hi, f0, s1, s2, s3 = attn_bwd(
        x, fars, rl, pair_b, r_b, p_b, at_b, xg
    )
    sum_aa = scatter_pair(do_a, dt_a, (1, 2))
    sum_ab = scatter_pair(do_b, dt_b, (2, 1))
    to_left = lax.ppermute(lo, "tensor", down_one)
    to_right = lax.ppermute(hi, "tensor", up_one)
    f1, f2, f3 = [swap(s, "tensor", k) for s, k in ((s1, 1), (s2, 2), (s3, 3))]
    late = lax.optimization_barrier((nb_a, nb_b, fb_a, fb_b, f1, f2, f3))
    grad_tokens, gain_grads = post(
        own, to_right, to_left, f0, f1, f2, f3, res_grad, tok, pooled, member, gains, order
    )

    nb_a, nb_b, fb_a, fb_b, f1, f2, f3 = late
    near_table = jnp.dot(
        jnp.concatenate([nb_a, nb_b]).reshape(HEADS, 3 * BLOCK), local_onehot[0].astype(f32), precision=highest
    )
    far_hot = (far_at.reshape(-1)[:, None] == bucket).astype(f32)
    far_table = jnp.dot(
        jnp.concatenate([fb_a, fb_b]).reshape(HEADS, 16 * 128), far_hot, precision=highest
    )
    table_part = jnp.concatenate(
        [near_table.reshape(4, 3 * BUCKETS), far_table.reshape(4, 3 * BUCKETS)], axis=1
    )
    gain_part = jnp.stack([gain_grads[0], gain_ff_grad[0], gain_grads[1]])
    gain_part = gain_part.reshape(3, count, width).transpose(1, 0, 2).reshape(count, 3 * width)
    small = jnp.concatenate(
        [
            jnp.broadcast_to(gain_part[None], (4, count, 3 * width)),
            jnp.broadcast_to(table_part[:, None], (4, count, 6 * BUCKETS)),
        ],
        axis=2,
    )
    for bit in [0, 2, 1] + high_bits()[::-1]:
        half = small.shape[1] // 2
        small = small[:, :half] + swap(small[:, half:], "fsdp", 1 << bit)
    small = scatter_tensor(small)[0]
    gain_sum = small[: 3 * width].reshape(3, width)
    table_sum = small[3 * width :].reshape(2, 3, BUCKETS).transpose(0, 2, 1)

    ff_sum = scatter_tensor([sum_fa[0], sum_fa[1], sum_fb[0], sum_fb[1]])
    at_sum = scatter_tensor([sum_aa[0], sum_aa[1], sum_ab[0], sum_ab[1]])
    col = lambda n: at_sum[:, n * 64 : n * 64 + 64]
    grad_query = jnp.concatenate([at_sum[:, 0:128], col(6)], axis=1)
    grad_key = jnp.concatenate([at_sum[:, 128:256], col(8)], axis=1)
    grad_value = jnp.concatenate([at_sum[:, 256:384], col(7)], axis=1)
    grad_out_w = jnp.concatenate([at_sum[:, 640:768], col(9)], axis=1).T
    return (
        output,
        grad_tokens,
        gain_sum[0],
        gain_sum[1],
        gain_sum[2],
        grad_query,
        grad_key,
        grad_value,
        grad_out_w,
        ff_sum[:, 0:FFS],
        ff_sum[:, FFS : 2 * FFS],
        ff_sum[:, 2 * FFS : 3 * FFS].T,
        table_sum[0],
        table_sum[1],
    )


def solution(mesh):
    return jax.shard_map(
        inner,
        mesh=mesh,
        in_specs=(
            P(("fsdp", "tensor"), None),
            P("fsdp"),
            P("fsdp"),
            P("fsdp"),
            P("fsdp", "tensor"),
            P("fsdp", "tensor"),
            P("fsdp", "tensor"),
            P("tensor", "fsdp"),
            P("fsdp", "tensor"),
            P("fsdp", "tensor"),
            P("tensor", "fsdp"),
            P(None, "tensor"),
            P(None, "tensor"),
            P(),
            P(),
            P("fsdp", None),
            P(("fsdp", "tensor"), None),
        ),
        out_specs=(
            P(("fsdp", "tensor"), None),
            P(("fsdp", "tensor"), None),
            P("fsdp"),
            P("fsdp"),
            P("fsdp"),
            P("fsdp", "tensor"),
            P("fsdp", "tensor"),
            P("fsdp", "tensor"),
            P("tensor", "fsdp"),
            P("fsdp", "tensor"),
            P("fsdp", "tensor"),
            P("tensor", "fsdp"),
            P(None, "tensor"),
            P(None, "tensor"),
        ),
        check_vma=False,
    )
```

```python
import jax
import jax.numpy as jnp
from jax import lax
from jax.experimental import pallas as pl
from jax.experimental.pallas import tpu as pltpu
from jax.sharding import PartitionSpec as P


D = 768
HEADS = 12
BUCKETS = 32
BLOCK = 128
GBLOCK = 16
SLOTS = 64
ROWS = 256
FAR = 32
EXT = ROWS + 2 * BLOCK
ALL = EXT + 4 * FAR
KEYS = 3 * BLOCK + 4 * FAR
HALF = D // 2
FFS = 512
WIDE = 3 * FFS + D

f32 = jnp.float32
bf16 = jnp.bfloat16
tiny_eps = 1e-06
masked_score = -1e30


def dot(a, b):
    return lax.dot_general(a, b, (((1,), (0,)), ((), ())), preferred_element_type=f32)


def dot_nt(a, b):
    return lax.dot_general(a, b, (((1,), (1,)), ((), ())), preferred_element_type=f32)


def dot_tn(a, b):
    return lax.dot_general(a, b, (((0,), (0,)), ((), ())), preferred_element_type=f32)


def whole_spec(shape):
    return pl.BlockSpec(shape, lambda i: (0,) * len(shape))


def slab_spec(shape):
    return pl.BlockSpec((1,) + shape, lambda i: (i,) + (0,) * len(shape))


def shape_of(shape, dtype):
    return jax.ShapeDtypeStruct(shape, dtype)


def rsqrt_mean(v):
    return lax.rsqrt(jnp.mean(v * v, axis=-1, keepdims=True) + tiny_eps)


def row_term(v, r, gain, e):
    eg = e * gain
    return r * eg - v * (r * r * r) * jnp.mean(eg * v, axis=-1, keepdims=True)


def eye(rows, cols):
    at = lax.broadcasted_iota(jnp.int32, (rows, cols), 0)
    return (at == lax.broadcasted_iota(jnp.int32, (rows, cols), 1)).astype(bf16)


def pack_kernel(wq, wk, wv, wo, gate, up, down_t, out):
    rows = wq.shape[0]
    out_t = dot_nt(eye(rows, rows), wo[...]).astype(bf16)
    out[:, 0:FFS] = gate[...]
    out[:, FFS : 2 * FFS] = up[...]
    out[:, 2 * FFS : 3 * FFS] = down_t[...]
    at = 3 * FFS
    out[:, at : at + 128] = wq[:, 0:128]
    out[:, at + 128 : at + 256] = wk[:, 0:128]
    out[:, at + 256 : at + 384] = wv[:, 0:128]
    out[:, at + 384 : at + 512] = jnp.concatenate([wq[:, 128:192], wv[:, 128:192]], axis=1)
    out[:, at + 512 : at + 640] = jnp.concatenate([wk[:, 128:192], out_t[:, 128:192]], axis=1)
    out[:, at + 640 : at + 768] = out_t[:, 0:128]


def pack(*shards):
    return pl.pallas_call(
        pack_kernel, out_shape=shape_of((shards[0].shape[0], WIDE), bf16), name="pack"
    )(*shards)


def prep_kernel(left, tok, right, grad, order, gains, mem, tables, x, tokp, gop, pooled_ref, far):
    turn = order[...]
    gain = gains[0:1]
    for base, ref in ((0, left), (BLOCK, tok), (BLOCK + ROWS, right)):
        v = dot(ref[...], turn)
        x[base : base + ref.shape[0]] = (v * rsqrt_mean(v) * gain).astype(bf16)
        if ref is tok:
            tokp[...] = v.astype(bf16)
    gop[...] = dot(grad[...], turn).astype(bf16)
    pooled = dot(mem[...], x[BLOCK : BLOCK + ROWS])
    pooled_ref[...] = pooled
    rows = (pooled * rsqrt_mean(pooled) * gains[2:3]).astype(bf16)
    at = lax.broadcasted_iota(jnp.int32, rows.shape, 0)
    far[...] = jnp.where(at == FAR - 1, jnp.broadcast_to(tables[...], rows.shape), rows)


def prep(*args):
    return pl.pallas_call(
        prep_kernel,
        out_shape=[
            shape_of((EXT, D), bf16),
            shape_of((ROWS, D), bf16),
            shape_of((ROWS, D), bf16),
            shape_of((FAR, D), f32),
            shape_of((FAR, D), bf16),
        ],
        name="prep",
    )(*args)


def join(w_s, pieces, step):
    for n in range(len(pieces) // 8):

        @pl.when(step == n)
        def _(n=n):
            for k in range(8):
                w_s[k * 96 : k * 96 + 96, :] = pieces[8 * n + k][...]


attn_spec = pl.BlockSpec((96, D), lambda i: (0, 2))
ff_specs = [pl.BlockSpec((96, 3 * FFS), lambda i: (0, 0))] * 16


def keys_of(tile, c):
    return jnp.concatenate([tile[c * BLOCK : c * BLOCK + 3 * BLOCK], tile[EXT:ALL]], axis=0)


def fill_x(x_s, x, fars):
    x_s[0:EXT] = x[...]
    for n, ref in enumerate(fars):
        x_s[EXT + n * FAR : EXT + n * FAR + FAR] = ref[...]


def turned(value, back):
    at = lax.broadcasted_iota(jnp.int32, value.shape, 0)
    size = value.shape[1]
    for bit in range(7):
        step = 1 << bit
        moved = pltpu.roll(value, size - step if back else step, 1)
        value = jnp.where((at >> bit) & 1 == 1, moved, value)
    return value


def attn_fwd_kernel(base, last, *refs):
    x, f0, f1, f2, f3 = refs[:5]
    pieces = refs[5:21]
    near_at, far_at, tables, mask = refs[21:25]
    refs = refs[25:]
    if last:
        before, tok, gains = refs[:3]
        refs = refs[3:]
        res, nf, p_ref, r_ref, a_ref, acc, x_s, w_s = refs
    else:
        acc, p_ref, r_ref, a_ref, x_s, w_s = refs
    step = pl.program_id(0)

    @pl.when(step == 0)
    def _():
        fill_x(x_s, x, (f0, f1, f2, f3))

    join(w_s, pieces, step)
    r = dot(x_s[...], w_s[:, 0:640]).astype(bf16)
    r_ref[0] = r
    low = lax.broadcasted_iota(jnp.int32, (BLOCK, 128), 1) < 64
    zero = jnp.zeros((BLOCK, 128), bf16)
    near_index = near_at[...]
    far_index = far_at[...]
    parts = [[None] * 3, [None] * 3]
    for j in range(3):
        head = (base + step) * 3 + j
        diagonal = jnp.zeros((1, 3 * BLOCK), f32)
        slots = jnp.zeros((16, 128), f32)
        for n in range(BUCKETS):
            diagonal = jnp.where(near_index == n, tables[head, n], diagonal)
            slots = jnp.where(far_index == n, tables[HEADS + head, n], slots)
        near = turned(jnp.broadcast_to(diagonal, (BLOCK, 3 * BLOCK)), False)
        q_all = r[:, 0:128] if j < 2 else r[:, 384:512]
        k_all = r[:, 128:256] if j < 2 else r[:, 512:640]
        v_all = r[:, 256:384] if j < 2 else r[:, 384:512]
        for c in range(2):
            q = q_all[BLOCK + c * BLOCK : 2 * BLOCK + c * BLOCK]
            q = jnp.where(low, zero, q) if j == 1 else jnp.where(low, q, zero)
            far = jnp.broadcast_to(slots[c * 8 : c * 8 + 8][:, None], (8, GBLOCK, 128)).reshape(BLOCK, 128)
            s = dot_nt(q, keys_of(k_all, c)) + jnp.concatenate([near, far], axis=1) + mask[c]
            e = jnp.exp(s - jnp.max(s, axis=-1, keepdims=True))
            p = (e * (1.0 / jnp.sum(e, axis=-1, keepdims=True))).astype(bf16)
            p_ref[0, c * 3 + j] = p
            parts[c][j] = dot(p, keys_of(v_all, c))
    for c in range(2):
        a_ref[0, c * BLOCK : c * BLOCK + BLOCK] = jnp.concatenate(
            [jnp.where(low, 0.0, parts[c][2]), jnp.where(low, parts[c][0], parts[c][1])], axis=1
        ).astype(bf16)
    part = dot_nt(a_ref[0], w_s[:, 512:768])

    @pl.when(step == 0)
    def _():
        acc[...] = before[...] + part if last else part

    @pl.when(step > 0)
    def _():
        acc[...] += part

    if last:

        @pl.when(step == pl.num_programs(0) - 1)
        def _():
            v = tok[...].astype(f32) + acc[...]
            res[...] = v
            nf[...] = (v * rsqrt_mean(v) * gains[1:2]).astype(bf16)


x_specs = [whole_spec((EXT, D))] + [whole_spec((FAR, D))] * 4


def attn_fwd(base, x, fars, pieces, near_at, far_at, tables, mask, *rest):
    last = len(rest) > 0
    outs = [
        (slab_spec((6, BLOCK, KEYS)), shape_of((2, 6, BLOCK, KEYS), bf16)),
        (slab_spec((ALL, 640)), shape_of((2, ALL, 640), bf16)),
        (slab_spec((ROWS, 256)), shape_of((2, ROWS, 256), bf16)),
    ]
    wide = (whole_spec((ROWS, D)), shape_of((ROWS, D), f32))
    if last:
        outs = [wide, (whole_spec((ROWS, D)), shape_of((ROWS, D), bf16))] + outs
    else:
        outs = [wide] + outs
    return pl.pallas_call(
        lambda *refs: attn_fwd_kernel(base, last, *refs),
        grid=(2,),
        in_specs=x_specs
        + [attn_spec] * 16
        + [
            whole_spec((1, 3 * BLOCK)),
            whole_spec((16, 128)),
            pl.BlockSpec(memory_space=pltpu.SMEM),
            whole_spec((2, BLOCK, KEYS)),
        ]
        + ([whole_spec((ROWS, D)), whole_spec((ROWS, D)), whole_spec((8, D))] if last else []),
        out_specs=[o[0] for o in outs],
        out_shape=[o[1] for o in outs],
        scratch_shapes=([pltpu.VMEM((ROWS, D), f32)] if last else [])
        + [pltpu.VMEM((ALL, D), bf16), pltpu.VMEM((D, D), bf16)],
        name="attn_fwd_b" if last else "attn_fwd_a",
    )(x, *fars, *pieces, near_at, far_at, tables, mask, *rest)


def attn_bwd_kernel(slabs, more, last, *refs):
    x, f0, f1, f2, f3, rl = refs[:6]
    pieces = refs[6 : 6 + 8 * slabs]
    refs = refs[6 + 8 * slabs :]
    r_ref, p_ref, a_ref = refs[:3]
    refs = refs[3:]
    if more:
        before = refs[0]
        refs = refs[1:]
    if last:
        where_ref = refs[0]
        down, doth, near_ref, far_ref, own, fown, s1, s2, s3, s4, xg, x_s, w_s, dr_s = refs[1:]
    else:
        down, doth, near_ref, far_ref, xg, x_s, w_s, dr_s = refs
    step = pl.program_id(0)

    @pl.when(step == 0)
    def _():
        fill_x(x_s, x, (f0, f1, f2, f3))

    join(w_s, pieces, step)
    da = dot(rl[...], w_s[:, 512:768]).astype(bf16)
    low = lax.broadcasted_iota(jnp.int32, (BLOCK, 128), 1) < 64
    zero = jnp.zeros((BLOCK, 128), bf16)
    r = r_ref[0]
    dr_s[...] = jnp.zeros((ALL, 640), f32)

    def add_keys(n, c, value):
        lanes = slice(n * 128, n * 128 + 128)
        dr_s[c * BLOCK : c * BLOCK + 3 * BLOCK, lanes] += value[: 3 * BLOCK]
        dr_s[EXT:ALL, lanes] += value[3 * BLOCK :]

    near = [None, None, None]
    for c in range(2):
        rows = slice(BLOCK + c * BLOCK, 2 * BLOCK + c * BLOCK)
        held = None
        for j in range(3):
            p = p_ref[0, c * 3 + j]
            q = r[rows, 0:128] if j < 2 else r[rows, 384:512]
            q = jnp.where(low, zero, q) if j == 1 else jnp.where(low, q, zero)
            k = keys_of(r[:, 128:256] if j < 2 else r[:, 512:640], c)
            v = keys_of(r[:, 256:384] if j < 2 else r[:, 384:512], c)
            do = da[c * BLOCK : c * BLOCK + BLOCK, (128 if j < 2 else 0) : (256 if j < 2 else 128)]
            do = jnp.where(low, do, zero) if j == 0 else jnp.where(low, zero, do)
            wide = p.astype(f32)
            dp = dot_nt(do, v)
            ds = wide * (dp - jnp.sum(wide * dp, axis=-1, keepdims=True))
            near[j] = ds[:, : 3 * BLOCK] if c == 0 else near[j] + ds[:, : 3 * BLOCK]
            far_ref[0, j, c * 8 : c * 8 + 8] = jnp.sum(
                ds[:, 3 * BLOCK :].reshape(8, GBLOCK, 128), axis=1
            )
            dl = ds.astype(bf16)
            dq = dot(dl, k)
            add_keys(1 if j < 2 else 4, c, dot_tn(dl, q))
            add_keys(2 if j < 2 else 3, c, dot_tn(p, do))
            if j == 0:
                held = dq
            elif j == 1:
                dr_s[rows, 0:128] = jnp.where(low, held, dq)
            else:
                dr_s[rows, 384:512] += jnp.where(low, dq, 0.0)
    for j in range(3):
        near_ref[0, j : j + 1] = jnp.sum(turned(near[j], True), axis=0, keepdims=True)
    dr = dr_s[...].astype(bf16)
    part = dot_nt(dr, w_s[:, 0:640])

    @pl.when(step == 0)
    def _():
        xg[...] = before[...] + part if more else part

    @pl.when(step > 0)
    def _():
        xg[...] += part

    for ref, base in ((down, 0), (doth, HALF)):
        g = dot_tn(x_s[:, base : base + HALF], dr)
        go = dot_tn(rl[:, base : base + HALF], a_ref[0])
        ref[0, :, 0:512] = g[:, 0:512].astype(bf16)
        ref[0, :, 512:640] = (g[:, 512:640] + go[:, 0:128]).astype(bf16)
        ref[0, :, 640:768] = go[:, 128:256].astype(bf16)
    if last:

        @pl.when(step == pl.num_programs(0) - 1)
        def _():
            own[...] = xg[BLOCK : BLOCK + ROWS]
            fown[...] = xg[EXT : EXT + FAR]
            lo = xg[0:BLOCK].astype(bf16)
            hi = xg[BLOCK + ROWS : EXT].astype(bf16)
            odd = where_ref[0] > 0
            s1[0:BLOCK] = jnp.where(odd, lo, hi)
            s4[...] = jnp.where(odd, hi, lo)
            s1[BLOCK:] = xg[EXT + FAR : EXT + 2 * FAR].astype(bf16)
            s2[...] = xg[EXT + 2 * FAR : EXT + 3 * FAR].astype(bf16)
            s3[...] = xg[EXT + 3 * FAR : EXT + 4 * FAR].astype(bf16)


def attn_bwd(x, fars, rl, pieces, offset, r, p, a, *rest):
    slabs = len(pieces) // 8
    more = len(rest) > 0
    last = len(rest) > 1

    def part_spec(shape):
        return pl.BlockSpec((1,) + shape, lambda i: (i + offset,) + (0,) * len(shape))

    outs = [
        (slab_spec((HALF, D)), shape_of((slabs, HALF, D), bf16)),
        (slab_spec((HALF, D)), shape_of((slabs, HALF, D), bf16)),
        (slab_spec((3, 3 * BLOCK)), shape_of((slabs, 3, 3 * BLOCK), f32)),
        (slab_spec((3, 16, 128)), shape_of((slabs, 3, 16, 128), f32)),
    ]
    if last:
        for rows, dtype in (
            (ROWS, f32), (FAR, f32), (BLOCK + FAR, bf16), (FAR, bf16), (FAR, bf16), (BLOCK, bf16),
        ):
            outs.append((whole_spec((rows, D)), shape_of((rows, D), dtype)))
    else:
        outs.append((whole_spec((ALL, D)), shape_of((ALL, D), f32)))
    return pl.pallas_call(
        lambda *refs: attn_bwd_kernel(slabs, more, last, *refs),
        grid=(slabs,),
        in_specs=x_specs
        + [whole_spec((ROWS, D))]
        + [attn_spec] * (8 * slabs)
        + [part_spec((ALL, 640)), part_spec((6, BLOCK, KEYS)), part_spec((ROWS, 256))]
        + ([whole_spec((ALL, D))] if more else [])
        + ([pl.BlockSpec(memory_space=pltpu.SMEM)] if last else []),
        out_specs=[o[0] for o in outs],
        out_shape=[o[1] for o in outs],
        scratch_shapes=([pltpu.VMEM((ALL, D), f32)] if last else [])
        + [pltpu.VMEM((ALL, D), bf16), pltpu.VMEM((D, D), bf16), pltpu.VMEM((ALL, 640), f32)],
    )(x, *fars, rl, *pieces, r, p, a, *rest)


def ff_kernel(last, *refs):
    nf, go = refs[:2]
    pieces = refs[2:18]
    refs = refs[18:]
    if last:
        out_a, ng_a, res, gains, order = refs[:5]
        down, doth, output, res_grad, rl, gain_grad, out_acc, ng_acc, w_s = refs[5:]
    else:
        down, doth, out_acc, ng_acc, w_s = refs
    step = pl.program_id(0)
    join(w_s, pieces, step)
    gate = dot(nf[...], w_s[:, 0:FFS])
    up = dot(nf[...], w_s[:, FFS : 2 * FFS])
    hg = dot(go[...], w_s[:, 2 * FFS : 3 * FFS])
    root = 0.7978845608028654
    t = jnp.tanh(root * (gate + 0.044715 * gate * gate * gate))
    cdf = 0.5 * (1.0 + t)
    act = gate * cdf
    slope = cdf + 0.5 * gate * (1.0 - t * t) * (root * (1.0 + 3.0 * 0.044715 * gate * gate))
    hidden = (act * up).astype(bf16)
    both = jnp.concatenate([(hg * up * slope).astype(bf16), (hg * act).astype(bf16)], axis=1)
    out = dot_nt(hidden, w_s[:, 2 * FFS : 3 * FFS])
    ng = dot_nt(both, w_s[:, 0 : 2 * FFS])

    @pl.when(step == 0)
    def _():
        out_acc[...] = out_a[...] + out if last else out
        ng_acc[...] = ng_a[...] + ng if last else ng

    @pl.when(step > 0)
    def _():
        out_acc[...] += out
        ng_acc[...] += ng

    for ref, base in ((down, 0), (doth, HALF)):
        ref[0, :, 0 : 2 * FFS] = dot_tn(nf[:, base : base + HALF], both).astype(bf16)
        ref[0, :, 2 * FFS : 3 * FFS] = dot_tn(go[:, base : base + HALF], hidden).astype(bf16)
    if last:

        @pl.when(step == pl.num_programs(0) - 1)
        def _():
            v = res[...]
            r = rsqrt_mean(v)
            e = ng_acc[...]
            output[...] = dot_nt((v + out_acc[...]).astype(bf16), order[...]).astype(bf16)
            total = go[...].astype(f32) + row_term(v, r, gains[1:2], e)
            res_grad[...] = total
            rl[...] = total.astype(bf16)
            gain_grad[...] = jnp.sum(e * v * r, axis=0, keepdims=True)


def ff_both(nf, go, pieces, *rest):
    last = len(rest) > 0
    wide = (whole_spec((ROWS, D)), shape_of((ROWS, D), f32))
    narrow = (whole_spec((ROWS, D)), shape_of((ROWS, D), bf16))
    outs = [(slab_spec((HALF, 3 * FFS)), shape_of((2, HALF, 3 * FFS), bf16))] * 2
    if last:
        outs = outs + [narrow, wide, narrow, (whole_spec((1, D)), shape_of((1, D), f32))]
    else:
        outs = outs + [wide, wide]
    return pl.pallas_call(
        lambda *refs: ff_kernel(last, *refs),
        grid=(2,),
        in_specs=[whole_spec((ROWS, D))] * 2
        + ff_specs
        + ([whole_spec((ROWS, D))] * 3 + [whole_spec((8, D)), whole_spec((D, D))] if last else []),
        out_specs=[o[0] for o in outs],
        out_shape=[o[1] for o in outs],
        scratch_shapes=([pltpu.VMEM((ROWS, D), f32)] * 2 if last else []) + [pltpu.VMEM((D, 3 * FFS), bf16)],
        name="ff_a" if last else "ff_b",
    )(nf, go, *pieces, *rest)


def split3(value):
    parts = []
    for _ in range(3):
        parts.append(value.astype(bf16))
        value = value - parts[-1].astype(f32)
    return parts


def post_kernel(
    where_ref, own, f0, r1, r2, r3, r4, res_grad, tok, pooled, mem, gains, order, gain_ff,
    near_0, near_1, near_b, far_0, far_1, far_b, near_at, far_at, grad, small,
):
    e = f0[...] + r1[BLOCK:].astype(f32) + r2[...].astype(f32) + r3[...].astype(f32)
    v = pooled[...]
    r = rsqrt_mean(v)
    spread = row_term(v, r, gains[2:3], e)
    gain_global = jnp.sum(e * v * r, axis=0, keepdims=True)
    odd = where_ref[0] > 0
    near = r1[0:BLOCK].astype(f32)
    other = jnp.where(where_ref[1] > 0, r4[...].astype(f32), 0.0)
    wide = own[...] + jnp.concatenate(
        [jnp.where(odd, near, other), jnp.where(odd, other, near)], axis=0
    )
    for part in split3(spread):
        wide = wide + dot_tn(mem[...], part)
    v = tok[...].astype(f32)
    r = rsqrt_mean(v)
    rest = res_grad[...] + row_term(v, r, gains[0:1], wide)
    sums = jnp.concatenate(
        [jnp.sum(wide * v * r, axis=0, keepdims=True), gain_ff[...], gain_global, jnp.zeros((5, D), f32)]
    )
    total = jnp.zeros((ROWS, D), f32)
    gain_sums = jnp.zeros((8, D), f32)
    for part, gain_part in zip(split3(rest), split3(sums)):
        total = total + dot_nt(part, order[...])
        gain_sums = gain_sums + dot_nt(gain_part, order[...])
    grad[...] = total
    small[0:8] = gain_sums
    bucket = lax.broadcasted_iota(jnp.int32, (BUCKETS, 3 * BLOCK), 0)
    near_hot = (jnp.broadcast_to(near_at[...], bucket.shape) == bucket).astype(bf16)
    far_hot = [
        (jnp.broadcast_to(far_at[a : a + 1], (BUCKETS, 128)) == bucket[:, 0:128]).astype(bf16) for a in range(16)
    ]
    at = lax.broadcasted_iota(jnp.int32, (16, 3), 0)
    col = lax.broadcasted_iota(jnp.int32, (16, 3), 1)
    near_of = (near_0[0], near_1[0], near_b[0], near_b[1])
    far_of = ((far_0, 0), (far_1, 0), (far_b, 0), (far_b, 1))
    near_sum = jnp.zeros((16, BUCKETS), f32)
    far_sum = jnp.zeros((16, BUCKETS), f32)
    for k in range(4):
        place = (at == col + 3 * (where_ref[2] ^ k)).astype(bf16)
        near_table = sum(dot_nt(part, near_hot) for part in split3(near_of[k]))
        far_table = jnp.zeros((3, BUCKETS), f32)
        for a in range(16):
            far_grad = far_of[k][0][far_of[k][1], :, a]
            far_table = far_table + sum(dot_nt(part, far_hot[a]) for part in split3(far_grad))
        near_sum = near_sum + sum(dot(place, part) for part in split3(near_table))
        far_sum = far_sum + sum(dot(place, part) for part in split3(far_table))
    small[8:24] = jnp.zeros((16, D), f32)
    small[8:24, 0:BUCKETS] = near_sum
    small[8:24, 128 : 128 + BUCKETS] = far_sum


def post(*args):
    in_vmem = pl.BlockSpec(memory_space=pltpu.VMEM)
    return pl.pallas_call(
        post_kernel,
        in_specs=[pl.BlockSpec(memory_space=pltpu.SMEM)] + [in_vmem] * (len(args) - 1),
        out_shape=[shape_of((ROWS, D), f32), shape_of((24, D), f32)],
        name="post",
    )(*args)


def unpack_kernel(s0, s1, s2, s3, q, k, v, o):
    wide = s0[...].astype(f32) + s1[...].astype(f32) + s2[...].astype(f32) + s3[...].astype(f32)
    q[:, 0:128] = wide[:, 0:128]
    k[:, 0:128] = wide[:, 128:256]
    v[:, 0:128] = wide[:, 256:384]
    q[:, 128:192] = wide[:, 384:448]
    v[:, 128:192] = wide[:, 448:512]
    k[:, 128:192] = wide[:, 512:576]
    o[:, 128:192] = wide[:, 576:640]
    o[:, 0:128] = wide[:, 640:768]


def unpack(*slabs):
    return pl.pallas_call(
        unpack_kernel, out_shape=[shape_of((slabs[0].shape[0], 192), f32)] * 4, name="unpack"
    )(*slabs)


def swap(x, axis, mask):
    size = lax.axis_size(axis)
    return lax.ppermute(x, axis, [(i, i ^ mask) for i in range(size)])


def high_bits():
    return list(range(3, lax.axis_size("fsdp").bit_length() - 1))


def near_swaps(x):
    got = [x]
    for n in (1, 2, 3):
        got.append(swap(x, "fsdp", n << 1))
    return got


def gather_high(shard):
    for bit in high_bits():
        shard = jnp.concatenate([shard, swap(shard, "fsdp", 1 << bit)], axis=0)
    return shard


def gather_tensor(x):
    got = []
    for k in (1, 2, 3):
        got.append(swap(x, "tensor", k))
    return got


def scatter_pair(sources):
    dtype = sources[0][0].dtype
    came = []
    for _, oth in sources:
        came.append(swap(oth, "fsdp", 1))

    def piece(n):
        rows = slice(n * 96, n * 96 + 96)
        return jnp.concatenate(
            [own[:, rows].astype(f32) + got[:, rows].astype(f32) for (own, _), got in zip(sources, came)]
        )

    total = piece(0)
    for n in (1, 2, 3):
        total = total + swap(piece(n).astype(dtype), "fsdp", n << 1).astype(f32)
    total = total.astype(dtype)
    for bit in high_bits()[::-1]:
        half = total.shape[1] // 2
        total = total[:, :half] + swap(total[:, half:], "fsdp", 1 << bit)
    return total


def scatter_tensor(slabs):
    got = [slabs[0]]
    for k in (1, 2, 3):
        got.append(swap(slabs[k], "tensor", k))
    return got


def inner(
    tokens, ln_attn, ln_ff, ln_global, w_query, w_key, w_value, w_out, wi_gate, wi_up, wo_ff,
    table_local, table_global, local_onehot, global_onehot, segment, grad_out,
):
    count = lax.axis_size("fsdp")
    width = D // count
    f = lax.axis_index("fsdp")
    z = lax.axis_index("tensor")
    last = lax.axis_size("tensor") - 1
    up_one = [(i, i + 1) for i in range(last)]
    down_one = [(i + 1, i) for i in range(last)]

    gains = jnp.stack([ln_attn, ln_ff, ln_global])[:, None, :]
    for bit in high_bits():
        gains = jnp.concatenate([gains, swap(gains, "fsdp", 1 << bit)], axis=1)
    gains = jnp.concatenate(near_swaps(gains), axis=1)
    gains = jnp.concatenate([gains, swap(gains, "fsdp", 1)], axis=1)
    gains = jnp.pad(gains.reshape(3, D).astype(f32), ((0, 5), (0, 0)))
    left = lax.ppermute(tokens[ROWS - BLOCK :], "tensor", up_one)
    right = lax.ppermute(tokens[:BLOCK], "tensor", down_one)

    shard = gather_high(pack(w_query, w_key, w_value, w_out, wi_gate, wi_up, wo_ff.T))
    slabs = [shard] + gather_tensor(shard)
    tables = jnp.concatenate([table_local.T.reshape(1, -1), table_global.T.reshape(1, -1)], axis=1)
    tables = jnp.pad(tables, ((0, 0), (0, D - tables.shape[1])))

    true_at = jnp.arange(D, dtype=jnp.int32)
    piece = true_at // 96
    high = (true_at % 96) // width
    relative = (piece // 4) | ((piece & 3) << 1) | (high << 3)
    source = (f ^ relative) * width + true_at % width
    order = (true_at[:, None] == source[None, :]).astype(bf16)

    seg_row = segment[0]
    parts = seg_row.reshape(4, ROWS)
    rel = jnp.arange(4, dtype=jnp.int32) ^ z
    seg_rel = jnp.take(parts, rel, axis=0)
    here = jnp.arange(ROWS, dtype=jnp.int32)
    starts = (here % GBLOCK == 0)[None] | (
        seg_rel != jnp.concatenate([seg_rel[:, :1], seg_rel[:, :-1]], axis=1)
    )
    triangle = (here[:, None] <= here[None, :]).astype(bf16)
    piece_rel = dot(starts.astype(bf16), triangle).astype(jnp.int32) - 1
    is_in = piece_rel[:, None, :] == jnp.arange(FAR, dtype=jnp.int32)[:, None]
    slot_rel = rel[:, None] * (ROWS // GBLOCK) + here[None] // GBLOCK
    piece_doc = jnp.max(jnp.where(is_in, seg_rel[:, None, :], -1), axis=2).reshape(4 * FAR)
    piece_slot = jnp.max(jnp.where(is_in, slot_rel[:, None, :], -1), axis=2).reshape(4 * FAR)
    member = is_in[0].astype(bf16)

    x, tok, go, pooled, far_rows = prep(left, tokens, right, grad_out, order, gains, member, tables)
    fars = [far_rows] + gather_tensor(far_rows)

    tables = jnp.stack([far[FAR - 1, : 6 * BUCKETS] for far in fars])
    tables = tables.reshape(4, 2, 3, BUCKETS).transpose(1, 0, 2, 3).reshape(2 * HEADS, BUCKETS).astype(f32)

    padded = jnp.concatenate([jnp.full((BLOCK,), -1, jnp.int32), seg_row, jnp.full((BLOCK,), -1, jnp.int32)])
    seg_ext = lax.dynamic_slice(padded, (z * ROWS,), (EXT,))
    seg_own = seg_ext[BLOCK : BLOCK + ROWS].reshape(2, BLOCK)
    seg_keys = jnp.stack([seg_ext[: 3 * BLOCK], seg_ext[BLOCK:]])
    offset = jnp.arange(3 * BLOCK, dtype=jnp.int32)[None] - BLOCK - jnp.arange(BLOCK, dtype=jnp.int32)[:, None]
    near_ok = (jnp.abs(offset) < BLOCK)[None] & (seg_own[:, :, None] == seg_keys[:, None, :])
    far_ok = seg_own[:, :, None] == piece_doc[None, None, :]
    mask = jnp.where(jnp.concatenate([near_ok, far_ok], axis=2), 0.0, masked_score).astype(f32)
    bucket = jnp.arange(BUCKETS, dtype=jnp.int32)
    near_at = jnp.sum(local_onehot[0] * bucket, axis=1)[None]
    own_hot = lax.dynamic_slice(global_onehot, (z * 16, 0, 0), (16, SLOTS, BUCKETS))
    slot_at = jnp.sum(own_hot * bucket, axis=2)
    slot_is = piece_slot[None, :] == jnp.arange(SLOTS, dtype=jnp.int32)[:, None]
    far_at = dot(slot_at.astype(bf16), slot_is.astype(bf16)).astype(jnp.int32)

    small_work = (mask, near_at, far_at, tables)
    whole = []
    for n, slab in enumerate(slabs):
        own_pieces = near_swaps(slab)
        if n == 1:
            own_pieces, (mask, near_at, far_at, tables) = lax.optimization_barrier((own_pieces, small_work))
        whole.append(own_pieces + [swap(piece, "fsdp", 1) for piece in own_pieces])
    pair_a = whole[0] + whole[1]
    pair_b = whole[2] + whole[3]

    acc, p_a, r_a, at_a = attn_fwd(0, x, fars, pair_a, near_at, far_at, tables, mask)
    residual, nf, p_b, r_b, at_b = attn_fwd(
        2, x, fars, pair_b, near_at, far_at, tables, mask, acc, tok, gains
    )
    fo_b, ft_b, out_b, ng_b = ff_both(nf, go, pair_b)
    fo_a, ft_a, output, res_grad, rl, gain_ff = ff_both(
        nf, go, pair_a, out_b, ng_b, residual, gains, order
    )
    sum_fb = scatter_pair([(fo_b, ft_b)])
    sum_fa = scatter_pair([(fo_a, ft_a)])
    where = jnp.stack([z & 1, ((z == 1) | (z == 2)).astype(jnp.int32), z]).astype(jnp.int32)
    do_b, dt_b, nb_b, fb_b, xg = attn_bwd(x, fars, rl, pair_b, 0, r_b, p_b, at_b)
    do_1, dt_1, nb_1, fb_1, xg = attn_bwd(x, fars, rl, whole[1], 1, r_a, p_a, at_a, xg)
    do_0, dt_0, nb_0, fb_0, own, f0, s1, s2, s3, s4 = attn_bwd(x, fars, rl, whole[0], 0, r_a, p_a, at_a, xg, where)
    sum_ab = scatter_pair([(do_b, dt_b)])
    sum_aa = scatter_pair([(do_0, dt_0), (do_1, dt_1)])
    got = []
    for k, sent in ((1, s1), (2, s2), (3, s3)):
        got.append(swap(sent, "tensor", k))
    got.append(lax.ppermute(s4, "tensor", [(1, 2), (2, 1)]))
    grad_tokens, small = post(
        where, own, f0, *got, res_grad, tok, pooled, member, gains, order, gain_ff,
        nb_0, nb_1, nb_b, fb_0, fb_1, fb_b, near_at, far_at,
    )
    got = [small] + gather_tensor(small)
    small = (got[0] + got[1]) + (got[2] + got[3])
    small = small + swap(small, "fsdp", 1)
    got = near_swaps(small)
    small = (got[0] + got[1]) + (got[2] + got[3])
    for bit in high_bits():
        small = small + swap(small, "fsdp", 1 << bit)
    gain_sum = lax.dynamic_slice(small, (0, f * width), (3, width))
    table_sum = lax.dynamic_slice(small, (8 + 3 * z, 0), (3, 256))

    parts = scatter_tensor([sum_fa[0], sum_fa[1], sum_fb[0], sum_fb[1]])
    ff_sum = sum(part.astype(f32) for part in parts)
    grad_query, grad_key, grad_value, grad_out_t = unpack(*scatter_tensor([sum_aa[0], sum_aa[1], sum_ab[0], sum_ab[1]]))
    return (
        output,
        grad_tokens,
        gain_sum[0],
        gain_sum[1],
        gain_sum[2],
        grad_query,
        grad_key,
        grad_value,
        grad_out_t.T,
        ff_sum[:, 0:FFS],
        ff_sum[:, FFS : 2 * FFS],
        ff_sum[:, 2 * FFS : 3 * FFS].T,
        table_sum[:, 0:BUCKETS].T,
        table_sum[:, 128 : 128 + BUCKETS].T,
    )


def solution(mesh):
    return jax.shard_map(
        inner,
        mesh=mesh,
        in_specs=(
            P(("fsdp", "tensor"), None),
            P("fsdp"),
            P("fsdp"),
            P("fsdp"),
            P("fsdp", "tensor"),
            P("fsdp", "tensor"),
            P("fsdp", "tensor"),
            P("tensor", "fsdp"),
            P("fsdp", "tensor"),
            P("fsdp", "tensor"),
            P("tensor", "fsdp"),
            P(None, "tensor"),
            P(None, "tensor"),
            P(),
            P(),
            P("fsdp", None),
            P(("fsdp", "tensor"), None),
        ),
        out_specs=(
            P(("fsdp", "tensor"), None),
            P(("fsdp", "tensor"), None),
            P("fsdp"),
            P("fsdp"),
            P("fsdp"),
            P("fsdp", "tensor"),
            P("fsdp", "tensor"),
            P("fsdp", "tensor"),
            P("tensor", "fsdp"),
            P("fsdp", "tensor"),
            P("fsdp", "tensor"),
            P("tensor", "fsdp"),
            P(None, "tensor"),
            P(None, "tensor"),
        ),
        check_vma=False,
    )
```

```python
import jax
import jax.numpy as jnp
from jax import lax
from jax.experimental import pallas as pl
from jax.experimental.pallas import tpu as pltpu
from jax.sharding import PartitionSpec as P


D = 768
HEADS = 12
BUCKETS = 32
BLOCK = 128
GBLOCK = 16
SLOTS = 64
ROWS = 256
FAR = 32
EXT = ROWS + 2 * BLOCK
ALL = EXT + 4 * FAR
KEYS = 3 * BLOCK + 4 * FAR
HALF = D // 2
FFS = 512
WIDE = 3 * FFS + D

f32 = jnp.float32
bf16 = jnp.bfloat16
tiny_eps = 1e-06
masked_score = -1e30


def dot(a, b):
    return lax.dot_general(a, b, (((1,), (0,)), ((), ())), preferred_element_type=f32)


def dot_nt(a, b):
    return lax.dot_general(a, b, (((1,), (1,)), ((), ())), preferred_element_type=f32)


def dot_tn(a, b):
    return lax.dot_general(a, b, (((0,), (0,)), ((), ())), preferred_element_type=f32)


def whole_spec(shape):
    return pl.BlockSpec(shape, lambda i: (0,) * len(shape))


def slab_spec(shape):
    return pl.BlockSpec((1,) + shape, lambda i: (i,) + (0,) * len(shape))


def shape_of(shape, dtype):
    return jax.ShapeDtypeStruct(shape, dtype)


def rsqrt_mean(v):
    return lax.rsqrt(jnp.mean(v * v, axis=-1, keepdims=True) + tiny_eps)


def row_term(v, r, gain, e):
    eg = e * gain
    return r * eg - v * (r * r * r) * jnp.mean(eg * v, axis=-1, keepdims=True)


def eye(rows, cols):
    at = lax.broadcasted_iota(jnp.int32, (rows, cols), 0)
    return (at == lax.broadcasted_iota(jnp.int32, (rows, cols), 1)).astype(bf16)


def pack_kernel(wq, wk, wv, wo, gate, up, down_t, out):
    rows = wq.shape[0]
    out_t = dot_nt(eye(rows, rows), wo[...]).astype(bf16)
    out[:, 0:FFS] = gate[...]
    out[:, FFS : 2 * FFS] = up[...]
    out[:, 2 * FFS : 3 * FFS] = down_t[...]
    at = 3 * FFS
    out[:, at : at + 128] = wq[:, 0:128]
    out[:, at + 128 : at + 256] = wk[:, 0:128]
    out[:, at + 256 : at + 384] = wv[:, 0:128]
    out[:, at + 384 : at + 512] = jnp.concatenate([wq[:, 128:192], wv[:, 128:192]], axis=1)
    out[:, at + 512 : at + 640] = jnp.concatenate([wk[:, 128:192], out_t[:, 128:192]], axis=1)
    out[:, at + 640 : at + 768] = out_t[:, 0:128]


def pack(*shards):
    return pl.pallas_call(
        pack_kernel, out_shape=shape_of((shards[0].shape[0], WIDE), bf16), name="pack"
    )(*shards)


def prep_kernel(tok, grad, order, gains, mem, tables, x, tokp, gop, pooled_ref, far):
    turn = order[...]
    v = dot(tok[...], turn)
    x[...] = (v * rsqrt_mean(v) * gains[0:1]).astype(bf16)
    tokp[...] = v.astype(bf16)
    gop[...] = dot(grad[...], turn).astype(bf16)
    pooled = dot(mem[...], x[...])
    pooled_ref[...] = pooled
    rows = (pooled * rsqrt_mean(pooled) * gains[2:3]).astype(bf16)
    at = lax.broadcasted_iota(jnp.int32, rows.shape, 0)
    far[...] = jnp.where(at == FAR - 1, jnp.broadcast_to(tables[...], rows.shape), rows)


def prep(*args):
    return pl.pallas_call(
        prep_kernel,
        out_shape=[
            shape_of((ROWS, D), bf16),
            shape_of((ROWS, D), bf16),
            shape_of((ROWS, D), bf16),
            shape_of((FAR, D), f32),
            shape_of((FAR, D), bf16),
        ],
        name="prep",
    )(*args)


def edge_kernel(left, right, order, gains, edge):
    for n, ref in enumerate((left, right)):
        v = dot(ref[...], order[...])
        edge[n * BLOCK : n * BLOCK + BLOCK] = (v * rsqrt_mean(v) * gains[0:1]).astype(bf16)


def edge_rows(*args):
    return pl.pallas_call(edge_kernel, out_shape=shape_of((2 * BLOCK, D), bf16), name="edge")(*args)


def join(w_s, pieces, step):
    for n in range(len(pieces) // 8):

        @pl.when(step == n)
        def _(n=n):
            def rows(i, carry):
                for k in range(8):
                    w_s[pl.ds(pl.multiple_of(k * 96 + i * 16, 16), 16), :] = pieces[8 * n + k][
                        pl.ds(pl.multiple_of(i * 16, 16), 16), :
                    ]
                return carry

            lax.fori_loop(0, 6, rows, 0)


attn_spec = pl.BlockSpec((96, D), lambda i: (0, 2))
ff_specs = [pl.BlockSpec((96, 3 * FFS), lambda i: (0, 0))] * 16


def keys_of(tile, c):
    return jnp.concatenate([tile[c * BLOCK : c * BLOCK + 3 * BLOCK], tile[EXT:ALL]], axis=0)


def fill_x(x_s, x, fars):
    own, edge = x
    x_s[0:BLOCK] = edge[0:BLOCK]
    x_s[BLOCK : BLOCK + ROWS] = own[...]
    x_s[BLOCK + ROWS : EXT] = edge[BLOCK:]
    for n, ref in enumerate(fars):
        x_s[EXT + n * FAR : EXT + n * FAR + FAR] = ref[...]


def turned(value, back):
    at = lax.broadcasted_iota(jnp.int32, value.shape, 0)
    size = value.shape[1]
    for bit in range(7):
        step = 1 << bit
        moved = pltpu.roll(value, size - step if back else step, 1)
        value = jnp.where((at >> bit) & 1 == 1, moved, value)
    return value


def attn_fwd_kernel(base, last, *refs):
    x, f0, f1, f2, f3 = (refs[:2],) + refs[2:6]
    pieces = refs[6:22]
    near_at, far_at, tables, mask = refs[22:26]
    refs = refs[26:]
    if last:
        before, tok, gains = refs[:3]
        refs = refs[3:]
        res, nf, p_ref, r_ref, a_ref, acc, x_s, w_s = refs
    else:
        acc, p_ref, r_ref, a_ref, x_s, w_s = refs
    step = pl.program_id(0)

    @pl.when(step == 0)
    def _():
        fill_x(x_s, x, (f0, f1, f2, f3))

    join(w_s, pieces, step)
    r = dot(x_s[...], w_s[:, 0:640]).astype(bf16)
    r_ref[0] = r
    low = lax.broadcasted_iota(jnp.int32, (BLOCK, 128), 1) < 64
    zero = jnp.zeros((BLOCK, 128), bf16)
    near_index = near_at[...]
    far_index = far_at[...]
    parts = [[None] * 3, [None] * 3]
    for j in range(3):
        head = (base + step) * 3 + j
        diagonal = jnp.zeros((1, 3 * BLOCK), f32)
        slots = jnp.zeros((16, 128), f32)
        for n in range(BUCKETS):
            diagonal = jnp.where(near_index == n, tables[head, n], diagonal)
            slots = jnp.where(far_index == n, tables[HEADS + head, n], slots)
        near = turned(jnp.broadcast_to(diagonal, (BLOCK, 3 * BLOCK)), False)
        q_all = r[:, 0:128] if j < 2 else r[:, 384:512]
        k_all = r[:, 128:256] if j < 2 else r[:, 512:640]
        v_all = r[:, 256:384] if j < 2 else r[:, 384:512]
        for c in range(2):
            q = q_all[BLOCK + c * BLOCK : 2 * BLOCK + c * BLOCK]
            q = jnp.where(low, zero, q) if j == 1 else jnp.where(low, q, zero)
            far = jnp.broadcast_to(slots[c * 8 : c * 8 + 8][:, None], (8, GBLOCK, 128)).reshape(BLOCK, 128)
            s = dot_nt(q, keys_of(k_all, c)) + jnp.concatenate([near, far], axis=1) + mask[c]
            e = jnp.exp(s - jnp.max(s, axis=-1, keepdims=True))
            p = (e * (1.0 / jnp.sum(e, axis=-1, keepdims=True))).astype(bf16)
            p_ref[0, c * 3 + j] = p
            parts[c][j] = dot(p, keys_of(v_all, c))
    for c in range(2):
        a_ref[0, c * BLOCK : c * BLOCK + BLOCK] = jnp.concatenate(
            [jnp.where(low, 0.0, parts[c][2]), jnp.where(low, parts[c][0], parts[c][1])], axis=1
        ).astype(bf16)
    part = dot_nt(a_ref[0], w_s[:, 512:768])

    @pl.when(step == 0)
    def _():
        acc[...] = before[...] + part if last else part

    @pl.when(step > 0)
    def _():
        acc[...] += part

    if last:

        @pl.when(step == pl.num_programs(0) - 1)
        def _():
            v = tok[...].astype(f32) + acc[...]
            res[...] = v
            nf[...] = (v * rsqrt_mean(v) * gains[1:2]).astype(bf16)


x_specs = [whole_spec((ROWS, D)), whole_spec((2 * BLOCK, D))] + [whole_spec((FAR, D))] * 4


def attn_fwd(base, x, fars, pieces, near_at, far_at, tables, mask, *rest):
    last = len(rest) > 0
    outs = [
        (slab_spec((6, BLOCK, KEYS)), shape_of((2, 6, BLOCK, KEYS), bf16)),
        (slab_spec((ALL, 640)), shape_of((2, ALL, 640), bf16)),
        (slab_spec((ROWS, 256)), shape_of((2, ROWS, 256), bf16)),
    ]
    wide = (whole_spec((ROWS, D)), shape_of((ROWS, D), f32))
    if last:
        outs = [wide, (whole_spec((ROWS, D)), shape_of((ROWS, D), bf16))] + outs
    else:
        outs = [wide] + outs
    return pl.pallas_call(
        lambda *refs: attn_fwd_kernel(base, last, *refs),
        grid=(2,),
        in_specs=x_specs
        + [attn_spec] * 16
        + [
            whole_spec((1, 3 * BLOCK)),
            whole_spec((16, 128)),
            pl.BlockSpec(memory_space=pltpu.SMEM),
            whole_spec((2, BLOCK, KEYS)),
        ]
        + ([whole_spec((ROWS, D)), whole_spec((ROWS, D)), whole_spec((8, D))] if last else []),
        out_specs=[o[0] for o in outs],
        out_shape=[o[1] for o in outs],
        scratch_shapes=([pltpu.VMEM((ROWS, D), f32)] if last else [])
        + [pltpu.VMEM((ALL, D), bf16), pltpu.VMEM((D, D), bf16)],
        name="attn_fwd_b" if last else "attn_fwd_a",
    )(*x, *fars, *pieces, near_at, far_at, tables, mask, *rest)


def attn_bwd_kernel(slabs, more, last, *refs):
    x, f0, f1, f2, f3, rl = (refs[:2],) + refs[2:7]
    pieces = refs[7 : 7 + 8 * slabs]
    refs = refs[7 + 8 * slabs :]
    r_ref, p_ref, a_ref = refs[:3]
    refs = refs[3:]
    if more:
        before = refs[0]
        refs = refs[1:]
    if last:
        where_ref = refs[0]
        down, doth, near_ref, far_ref, own, fown, s1, s2, s3, s4, xg, x_s, w_s, dr_s = refs[1:]
    else:
        down, doth, near_ref, far_ref, xg, x_s, w_s, dr_s = refs
    step = pl.program_id(0)

    @pl.when(step == 0)
    def _():
        fill_x(x_s, x, (f0, f1, f2, f3))

    join(w_s, pieces, step)
    da = dot(rl[...], w_s[:, 512:768]).astype(bf16)
    low = lax.broadcasted_iota(jnp.int32, (BLOCK, 128), 1) < 64
    zero = jnp.zeros((BLOCK, 128), bf16)
    r = r_ref[0]
    dr_s[...] = jnp.zeros((ALL, 640), f32)

    def add_keys(n, c, value):
        lanes = slice(n * 128, n * 128 + 128)
        dr_s[c * BLOCK : c * BLOCK + 3 * BLOCK, lanes] += value[: 3 * BLOCK]
        dr_s[EXT:ALL, lanes] += value[3 * BLOCK :]

    near = [None, None, None]
    for c in range(2):
        rows = slice(BLOCK + c * BLOCK, 2 * BLOCK + c * BLOCK)
        held = None
        for j in range(3):
            p = p_ref[0, c * 3 + j]
            q = r[rows, 0:128] if j < 2 else r[rows, 384:512]
            q = jnp.where(low, zero, q) if j == 1 else jnp.where(low, q, zero)
            k = keys_of(r[:, 128:256] if j < 2 else r[:, 512:640], c)
            v = keys_of(r[:, 256:384] if j < 2 else r[:, 384:512], c)
            do = da[c * BLOCK : c * BLOCK + BLOCK, (128 if j < 2 else 0) : (256 if j < 2 else 128)]
            do = jnp.where(low, do, zero) if j == 0 else jnp.where(low, zero, do)
            wide = p.astype(f32)
            dp = dot_nt(do, v)
            ds = wide * (dp - jnp.sum(wide * dp, axis=-1, keepdims=True))
            near[j] = ds[:, : 3 * BLOCK] if c == 0 else near[j] + ds[:, : 3 * BLOCK]
            far_ref[0, j, c * 8 : c * 8 + 8] = jnp.sum(
                ds[:, 3 * BLOCK :].reshape(8, GBLOCK, 128), axis=1
            )
            dl = ds.astype(bf16)
            dq = dot(dl, k)
            add_keys(1 if j < 2 else 4, c, dot_tn(dl, q))
            add_keys(2 if j < 2 else 3, c, dot_tn(p, do))
            if j == 0:
                held = dq
            elif j == 1:
                dr_s[rows, 0:128] = jnp.where(low, held, dq)
            else:
                dr_s[rows, 384:512] += jnp.where(low, dq, 0.0)
    for j in range(3):
        near_ref[0, j : j + 1] = jnp.sum(turned(near[j], True), axis=0, keepdims=True)
    dr = dr_s[...].astype(bf16)
    part = dot_nt(dr, w_s[:, 0:640])

    @pl.when(step == 0)
    def _():
        xg[...] = before[...] + part if more else part

    @pl.when(step > 0)
    def _():
        xg[...] += part

    for ref, base in ((down, 0), (doth, HALF)):
        g = dot_tn(x_s[:, base : base + HALF], dr)
        go = dot_tn(rl[:, base : base + HALF], a_ref[0])
        ref[0, :, 0:512] = g[:, 0:512].astype(bf16)
        ref[0, :, 512:640] = (g[:, 512:640] + go[:, 0:128]).astype(bf16)
        ref[0, :, 640:768] = go[:, 128:256].astype(bf16)
    if last:

        @pl.when(step == pl.num_programs(0) - 1)
        def _():
            own[...] = xg[BLOCK : BLOCK + ROWS]
            fown[...] = xg[EXT : EXT + FAR]
            lo = xg[0:BLOCK].astype(bf16)
            hi = xg[BLOCK + ROWS : EXT].astype(bf16)
            odd = where_ref[0] > 0
            s1[0:BLOCK] = jnp.where(odd, lo, hi)
            s4[...] = jnp.where(odd, hi, lo)
            s1[BLOCK:] = xg[EXT + FAR : EXT + 2 * FAR].astype(bf16)
            s2[...] = xg[EXT + 2 * FAR : EXT + 3 * FAR].astype(bf16)
            s3[...] = xg[EXT + 3 * FAR : EXT + 4 * FAR].astype(bf16)


def attn_bwd(x, fars, rl, pieces, offset, r, p, a, *rest):
    slabs = len(pieces) // 8
    more = len(rest) > 0
    last = len(rest) > 1

    def part_spec(shape):
        return pl.BlockSpec((1,) + shape, lambda i: (i + offset,) + (0,) * len(shape))

    outs = [
        (slab_spec((HALF, D)), shape_of((slabs, HALF, D), bf16)),
        (slab_spec((HALF, D)), shape_of((slabs, HALF, D), bf16)),
        (slab_spec((3, 3 * BLOCK)), shape_of((slabs, 3, 3 * BLOCK), f32)),
        (slab_spec((3, 16, 128)), shape_of((slabs, 3, 16, 128), f32)),
    ]
    if last:
        for rows, dtype in (
            (ROWS, f32), (FAR, f32), (BLOCK + FAR, bf16), (FAR, bf16), (FAR, bf16), (BLOCK, bf16),
        ):
            outs.append((whole_spec((rows, D)), shape_of((rows, D), dtype)))
    else:
        outs.append((whole_spec((ALL, D)), shape_of((ALL, D), f32)))
    return pl.pallas_call(
        lambda *refs: attn_bwd_kernel(slabs, more, last, *refs),
        grid=(slabs,),
        in_specs=x_specs
        + [whole_spec((ROWS, D))]
        + [attn_spec] * (8 * slabs)
        + [part_spec((ALL, 640)), part_spec((6, BLOCK, KEYS)), part_spec((ROWS, 256))]
        + ([whole_spec((ALL, D))] if more else [])
        + ([pl.BlockSpec(memory_space=pltpu.SMEM)] if last else []),
        out_specs=[o[0] for o in outs],
        out_shape=[o[1] for o in outs],
        scratch_shapes=([pltpu.VMEM((ALL, D), f32)] if last else [])
        + [pltpu.VMEM((ALL, D), bf16), pltpu.VMEM((D, D), bf16), pltpu.VMEM((ALL, 640), f32)],
    )(*x, *fars, rl, *pieces, r, p, a, *rest)


def ff_kernel(last, *refs):
    nf, go = refs[:2]
    pieces = refs[2:18]
    refs = refs[18:]
    if last:
        out_a, ng_a, res, gains, order = refs[:5]
        down, doth, output, res_grad, rl, gain_grad, out_acc, ng_acc, w_s = refs[5:]
    else:
        down, doth, out_acc, ng_acc, w_s = refs
    step = pl.program_id(0)
    join(w_s, pieces, step)
    gate = dot(nf[...], w_s[:, 0:FFS])
    up = dot(nf[...], w_s[:, FFS : 2 * FFS])
    hg = dot(go[...], w_s[:, 2 * FFS : 3 * FFS])
    root = 0.7978845608028654
    t = jnp.tanh(root * (gate + 0.044715 * gate * gate * gate))
    cdf = 0.5 * (1.0 + t)
    act = gate * cdf
    slope = cdf + 0.5 * gate * (1.0 - t * t) * (root * (1.0 + 3.0 * 0.044715 * gate * gate))
    hidden = (act * up).astype(bf16)
    both = jnp.concatenate([(hg * up * slope).astype(bf16), (hg * act).astype(bf16)], axis=1)
    out = dot_nt(hidden, w_s[:, 2 * FFS : 3 * FFS])
    ng = dot_nt(both, w_s[:, 0 : 2 * FFS])

    @pl.when(step == 0)
    def _():
        out_acc[...] = out_a[...] + out if last else out
        ng_acc[...] = ng_a[...] + ng if last else ng

    @pl.when(step > 0)
    def _():
        out_acc[...] += out
        ng_acc[...] += ng

    for ref, base in ((down, 0), (doth, HALF)):
        ref[0, :, 0 : 2 * FFS] = dot_tn(nf[:, base : base + HALF], both).astype(bf16)
        ref[0, :, 2 * FFS : 3 * FFS] = dot_tn(go[:, base : base + HALF], hidden).astype(bf16)
    if last:

        @pl.when(step == pl.num_programs(0) - 1)
        def _():
            v = res[...]
            r = rsqrt_mean(v)
            e = ng_acc[...]
            output[...] = dot_nt((v + out_acc[...]).astype(bf16), order[...]).astype(bf16)
            total = go[...].astype(f32) + row_term(v, r, gains[1:2], e)
            res_grad[...] = total
            rl[...] = total.astype(bf16)
            gain_grad[...] = jnp.sum(e * v * r, axis=0, keepdims=True)


def ff_both(nf, go, pieces, *rest):
    last = len(rest) > 0
    wide = (whole_spec((ROWS, D)), shape_of((ROWS, D), f32))
    narrow = (whole_spec((ROWS, D)), shape_of((ROWS, D), bf16))
    outs = [(slab_spec((HALF, 3 * FFS)), shape_of((2, HALF, 3 * FFS), bf16))] * 2
    if last:
        outs = outs + [narrow, wide, narrow, (whole_spec((1, D)), shape_of((1, D), f32))]
    else:
        outs = outs + [wide, wide]
    return pl.pallas_call(
        lambda *refs: ff_kernel(last, *refs),
        grid=(2,),
        in_specs=[whole_spec((ROWS, D))] * 2
        + ff_specs
        + ([whole_spec((ROWS, D))] * 3 + [whole_spec((8, D)), whole_spec((D, D))] if last else []),
        out_specs=[o[0] for o in outs],
        out_shape=[o[1] for o in outs],
        scratch_shapes=([pltpu.VMEM((ROWS, D), f32)] * 2 if last else []) + [pltpu.VMEM((D, 3 * FFS), bf16)],
        name="ff_a" if last else "ff_b",
    )(nf, go, *pieces, *rest)


def split3(value):
    parts = []
    for _ in range(3):
        parts.append(value.astype(bf16))
        value = value - parts[-1].astype(f32)
    return parts


def post_kernel(
    where_ref, own, f0, r1, r2, r3, r4, res_grad, tok, pooled, mem, gains, order, gain_ff,
    near_0, near_1, near_b, far_0, far_1, far_b, near_at, far_at, grad, small,
):
    e = f0[...] + r1[BLOCK:].astype(f32) + r2[...].astype(f32) + r3[...].astype(f32)
    v = pooled[...]
    r = rsqrt_mean(v)
    spread = row_term(v, r, gains[2:3], e)
    gain_global = jnp.sum(e * v * r, axis=0, keepdims=True)
    odd = where_ref[0] > 0
    near = r1[0:BLOCK].astype(f32)
    other = jnp.where(where_ref[1] > 0, r4[...].astype(f32), 0.0)
    wide = own[...] + jnp.concatenate(
        [jnp.where(odd, near, other), jnp.where(odd, other, near)], axis=0
    )
    for part in split3(spread):
        wide = wide + dot_tn(mem[...], part)
    v = tok[...].astype(f32)
    r = rsqrt_mean(v)
    rest = res_grad[...] + row_term(v, r, gains[0:1], wide)
    sums = jnp.concatenate(
        [jnp.sum(wide * v * r, axis=0, keepdims=True), gain_ff[...], gain_global, jnp.zeros((5, D), f32)]
    )
    total = jnp.zeros((ROWS, D), f32)
    gain_sums = jnp.zeros((8, D), f32)
    for part, gain_part in zip(split3(rest), split3(sums)):
        total = total + dot_nt(part, order[...])
        gain_sums = gain_sums + dot_nt(gain_part, order[...])
    grad[...] = total
    small[0:8] = gain_sums
    bucket = lax.broadcasted_iota(jnp.int32, (BUCKETS, 3 * BLOCK), 0)
    near_hot = (jnp.broadcast_to(near_at[...], bucket.shape) == bucket).astype(bf16)
    far_hot = [
        (jnp.broadcast_to(far_at[a : a + 1], (BUCKETS, 128)) == bucket[:, 0:128]).astype(bf16) for a in range(16)
    ]
    near_grad = jnp.concatenate([near_0[0], near_1[0], near_b[0], near_b[1]], axis=0)
    far_of = [far_0.at[0], far_1.at[0], far_b.at[0], far_b.at[1]]
    near_table = sum(dot_nt(part, near_hot) for part in split3(near_grad))
    far_table = jnp.zeros((HEADS, BUCKETS), f32)
    for a in range(16):
        far_grad = jnp.concatenate([ref[:, a] for ref in far_of], axis=0)
        far_table = far_table + sum(dot_nt(part, far_hot[a]) for part in split3(far_grad))
    at = lax.broadcasted_iota(jnp.int32, (16, HEADS), 0)
    col = lax.broadcasted_iota(jnp.int32, (16, HEADS), 1)
    place = jnp.zeros((16, HEADS), f32)
    for k in range(4):
        place = jnp.where((col // 3 == k) & (at == col % 3 + 3 * (where_ref[2] ^ k)), 1.0, place)
    place = place.astype(bf16)
    near_sum = sum(dot(place, part) for part in split3(near_table))
    far_sum = sum(dot(place, part) for part in split3(far_table))
    small[8:24] = jnp.zeros((16, D), f32)
    small[8:24, 0:BUCKETS] = near_sum
    small[8:24, 128 : 128 + BUCKETS] = far_sum


def post(*args):
    in_vmem = pl.BlockSpec(memory_space=pltpu.VMEM)
    return pl.pallas_call(
        post_kernel,
        in_specs=[pl.BlockSpec(memory_space=pltpu.SMEM)] + [in_vmem] * (len(args) - 1),
        out_shape=[shape_of((ROWS, D), f32), shape_of((24, D), f32)],
        name="post",
    )(*args)


def unpack_kernel(s0, s1, s2, s3, q, k, v, o):
    wide = s0[...].astype(f32) + s1[...].astype(f32) + s2[...].astype(f32) + s3[...].astype(f32)
    q[:, 0:128] = wide[:, 0:128]
    k[:, 0:128] = wide[:, 128:256]
    v[:, 0:128] = wide[:, 256:384]
    q[:, 128:192] = wide[:, 384:448]
    v[:, 128:192] = wide[:, 448:512]
    k[:, 128:192] = wide[:, 512:576]
    out = jnp.concatenate([wide[:, 640:768], wide[:, 576:640]], axis=1)
    o[...] = out.T if o.shape[0] == 192 else out


def unpack(*slabs):
    rows = slabs[0].shape[0]
    turn = rows % 32 == 0
    q, k, v, o = pl.pallas_call(
        unpack_kernel,
        out_shape=[shape_of((rows, 192), f32)] * 3 + [shape_of((192, rows) if turn else (rows, 192), f32)],
        name="unpack",
    )(*slabs)
    return q, k, v, o if turn else o.T


def swap(x, axis, mask):
    size = lax.axis_size(axis)
    return lax.ppermute(x, axis, [(i, i ^ mask) for i in range(size)])


def high_bits():
    return list(range(3, lax.axis_size("fsdp").bit_length() - 1))


def near_swaps(x):
    got = [x]
    for n in (1, 2, 3):
        got.append(swap(x, "fsdp", n << 1))
    return got


def gather_high(shard):
    for bit in high_bits():
        shard = jnp.concatenate([shard, swap(shard, "fsdp", 1 << bit)], axis=0)
    return shard


def gather_tensor(x):
    got = []
    for k in (1, 2, 3):
        got.append(swap(x, "tensor", k))
    return got


def scatter_pair(sources, behind=None):
    dtype = sources[0][0].dtype
    came = []
    for _, oth in sources:
        came.append(swap(oth, "fsdp", 1))

    def piece(n):
        rows = slice(n * 96, n * 96 + 96)
        return jnp.concatenate(
            [own[:, rows].astype(f32) + got[:, rows].astype(f32) for (own, _), got in zip(sources, came)]
        )

    total = piece(0)
    sends = [piece(n).astype(dtype) for n in (1, 2, 3)]
    came = []
    for n in (1, 2, 3):
        came.append(swap(sends[n - 1], "fsdp", n << 1))
    if behind is not None:
        came, _ = lax.optimization_barrier((came, behind))
    total = total + came[0].astype(f32) + came[1].astype(f32) + came[2].astype(f32)
    total = total.astype(dtype)
    for bit in high_bits()[::-1]:
        half = total.shape[1] // 2
        total = total[:, :half] + swap(total[:, half:], "fsdp", 1 << bit)
    return total, sends


def scatter_tensor(slabs):
    got = [slabs[0]]
    for k in (1, 2, 3):
        got.append(swap(slabs[k], "tensor", k))
    return got


def inner(
    tokens, ln_attn, ln_ff, ln_global, w_query, w_key, w_value, w_out, wi_gate, wi_up, wo_ff,
    table_local, table_global, local_onehot, global_onehot, segment, grad_out,
):
    count = lax.axis_size("fsdp")
    width = D // count
    f = lax.axis_index("fsdp")
    z = lax.axis_index("tensor")
    last = lax.axis_size("tensor") - 1
    up_one = [(i, i + 1) for i in range(last)]
    down_one = [(i + 1, i) for i in range(last)]

    gains = jnp.stack([ln_attn, ln_ff, ln_global])[:, None, :]
    for bit in high_bits():
        gains = jnp.concatenate([gains, swap(gains, "fsdp", 1 << bit)], axis=1)
    gains = jnp.concatenate(near_swaps(gains), axis=1)
    gains = jnp.concatenate([gains, swap(gains, "fsdp", 1)], axis=1)
    gains = jnp.pad(gains.reshape(3, D).astype(f32), ((0, 5), (0, 0)))
    left = lax.ppermute(tokens[ROWS - BLOCK :], "tensor", up_one)
    right = lax.ppermute(tokens[:BLOCK], "tensor", down_one)

    shard = gather_high(pack(w_query, w_key, w_value, w_out, wi_gate, wi_up, wo_ff.T))
    slabs = [shard] + gather_tensor(shard)
    tables = jnp.concatenate([table_local.T.reshape(1, -1), table_global.T.reshape(1, -1)], axis=1)
    tables = jnp.pad(tables, ((0, 0), (0, D - tables.shape[1])))

    seg_row, near_hot, tables, gains, f_late = lax.optimization_barrier(
        (segment[0], local_onehot[0], tables, gains, f)
    )

    true_at = jnp.arange(D, dtype=jnp.int32)
    piece = true_at // 96
    high = (true_at % 96) // width
    relative = (piece // 4) | ((piece & 3) << 1) | (high << 3)
    source = (f_late ^ relative) * width + true_at % width
    order = (true_at[:, None] == source[None, :]).astype(bf16)

    parts = seg_row.reshape(4, ROWS)
    rel = jnp.arange(4, dtype=jnp.int32) ^ z
    seg_rel = jnp.take(parts, rel, axis=0)
    here = jnp.arange(ROWS, dtype=jnp.int32)
    starts = (here % GBLOCK == 0)[None] | (
        seg_rel != jnp.concatenate([seg_rel[:, :1], seg_rel[:, :-1]], axis=1)
    )
    triangle = (here[:, None] <= here[None, :]).astype(bf16)
    piece_rel = dot(starts.astype(bf16), triangle).astype(jnp.int32) - 1
    member = (piece_rel[0] == jnp.arange(FAR, dtype=jnp.int32)[:, None]).astype(bf16)
    own_hot = lax.dynamic_slice(global_onehot, (z * 16, 0, 0), (16, SLOTS, BUCKETS))
    is_in = piece_rel[:, None, :] == jnp.arange(FAR, dtype=jnp.int32)[:, None]
    slot_rel = rel[:, None] * (ROWS // GBLOCK) + here[None] // GBLOCK
    piece_doc = jnp.max(jnp.where(is_in, seg_rel[:, None, :], -1), axis=2).reshape(4 * FAR)
    piece_slot = jnp.max(jnp.where(is_in, slot_rel[:, None, :], -1), axis=2).reshape(4 * FAR)

    x_own, tok, go, pooled, far_rows = prep(tokens, grad_out, order, gains, member, tables)
    x = (x_own, edge_rows(left, right, order, gains))
    fars = [far_rows] + gather_tensor(far_rows)

    tables = jnp.stack([far[FAR - 1, : 6 * BUCKETS] for far in fars])
    tables = tables.reshape(4, 2, 3, BUCKETS).transpose(1, 0, 2, 3).reshape(2 * HEADS, BUCKETS).astype(f32)

    padded = jnp.concatenate([jnp.full((BLOCK,), -1, jnp.int32), seg_row, jnp.full((BLOCK,), -1, jnp.int32)])
    seg_ext = lax.dynamic_slice(padded, (z * ROWS,), (EXT,))
    seg_own = seg_ext[BLOCK : BLOCK + ROWS].reshape(2, BLOCK)
    seg_keys = jnp.stack([seg_ext[: 3 * BLOCK], seg_ext[BLOCK:]])
    offset = jnp.arange(3 * BLOCK, dtype=jnp.int32)[None] - BLOCK - jnp.arange(BLOCK, dtype=jnp.int32)[:, None]
    near_ok = (jnp.abs(offset) < BLOCK)[None] & (seg_own[:, :, None] == seg_keys[:, None, :])
    far_ok = seg_own[:, :, None] == piece_doc[None, None, :]
    mask = jnp.where(jnp.concatenate([near_ok, far_ok], axis=2), 0.0, masked_score).astype(f32)
    bucket = jnp.arange(BUCKETS, dtype=jnp.int32)
    near_at = jnp.sum(near_hot * bucket, axis=1)[None]
    slot_at = jnp.sum(own_hot * bucket, axis=2)
    slot_is = piece_slot[None, :] == jnp.arange(SLOTS, dtype=jnp.int32)[:, None]
    far_at = dot(slot_at.astype(bf16), slot_is.astype(bf16)).astype(jnp.int32)

    small_work = (mask, near_at, far_at, tables)
    whole = []
    for n, slab in enumerate(slabs):
        own_pieces = near_swaps(slab)
        if n == 1:
            own_pieces, (mask, near_at, far_at, tables) = lax.optimization_barrier((own_pieces, small_work))
        whole.append(own_pieces + [swap(piece, "fsdp", 1) for piece in own_pieces])
    pair_a = whole[0] + whole[1]
    pair_b = whole[2] + whole[3]

    acc, p_a, r_a, at_a = attn_fwd(0, x, fars, pair_a, near_at, far_at, tables, mask)
    residual, nf, p_b, r_b, at_b = attn_fwd(
        2, x, fars, pair_b, near_at, far_at, tables, mask, acc, tok, gains
    )
    fo_b, ft_b, out_b, ng_b = ff_both(nf, go, pair_b)
    fo_a, ft_a, output, res_grad, rl, gain_ff = ff_both(
        nf, go, pair_a, out_b, ng_b, residual, gains, order
    )
    sum_fb, _ = scatter_pair([(fo_b, ft_b)])
    sum_fa, _ = scatter_pair([(fo_a, ft_a)])
    where = jnp.stack([z & 1, ((z == 1) | (z == 2)).astype(jnp.int32), z]).astype(jnp.int32)
    do_b, dt_b, nb_b, fb_b, xg = attn_bwd(x, fars, rl, pair_b, 0, r_b, p_b, at_b)
    do_1, dt_1, nb_1, fb_1, xg = attn_bwd(x, fars, rl, whole[1], 1, r_a, p_a, at_a, xg)
    do_0, dt_0, nb_0, fb_0, own, f0, s1, s2, s3, s4 = attn_bwd(
        x, fars, rl, whole[0], 0, r_a, p_a, at_a, xg, where
    )
    sum_aa, sends = scatter_pair([(do_0, dt_0), (do_1, dt_1)])
    sum_ab, _ = scatter_pair([(do_b, dt_b)], sends)
    got = []
    for k, sent in ((1, s1), (2, s2), (3, s3)):
        got.append(swap(sent, "tensor", k))
    got.append(lax.ppermute(s4, "tensor", [(1, 2), (2, 1)]))
    grad_tokens, small = post(
        where, own, f0, *got, res_grad, tok, pooled, member, gains, order, gain_ff,
        nb_0, nb_1, nb_b, fb_0, fb_1, fb_b, near_at, far_at,
    )
    got = [small] + gather_tensor(small)
    small = (got[0] + got[1]) + (got[2] + got[3])
    small = small + swap(small, "fsdp", 1)
    got = near_swaps(small)
    small = (got[0] + got[1]) + (got[2] + got[3])
    for bit in high_bits():
        small = small + swap(small, "fsdp", 1 << bit)
    gain_sum = lax.dynamic_slice(small, (0, f * width), (3, width))
    table_sum = lax.dynamic_slice(small, (8 + 3 * z, 0), (3, 256))

    parts = scatter_tensor([sum_fa[0], sum_fa[1], sum_fb[0], sum_fb[1]])
    ff_sum = sum(part.astype(f32) for part in parts)
    grad_query, grad_key, grad_value, grad_w_out = unpack(
        *scatter_tensor([sum_aa[0], sum_aa[1], sum_ab[0], sum_ab[1]])
    )
    return (
        output,
        grad_tokens,
        gain_sum[0],
        gain_sum[1],
        gain_sum[2],
        grad_query,
        grad_key,
        grad_value,
        grad_w_out,
        ff_sum[:, 0:FFS],
        ff_sum[:, FFS : 2 * FFS],
        ff_sum[:, 2 * FFS : 3 * FFS].T,
        table_sum[:, 0:BUCKETS].T,
        table_sum[:, 128 : 128 + BUCKETS].T,
    )


def solution(mesh):
    return jax.shard_map(
        inner,
        mesh=mesh,
        in_specs=(
            P(("fsdp", "tensor"), None),
            P("fsdp"),
            P("fsdp"),
            P("fsdp"),
            P("fsdp", "tensor"),
            P("fsdp", "tensor"),
            P("fsdp", "tensor"),
            P("tensor", "fsdp"),
            P("fsdp", "tensor"),
            P("fsdp", "tensor"),
            P("tensor", "fsdp"),
            P(None, "tensor"),
            P(None, "tensor"),
            P(),
            P(),
            P("fsdp", None),
            P(("fsdp", "tensor"), None),
        ),
        out_specs=(
            P(("fsdp", "tensor"), None),
            P(("fsdp", "tensor"), None),
            P("fsdp"),
            P("fsdp"),
            P("fsdp"),
            P("fsdp", "tensor"),
            P("fsdp", "tensor"),
            P("fsdp", "tensor"),
            P("tensor", "fsdp"),
            P("fsdp", "tensor"),
            P("fsdp", "tensor"),
            P("tensor", "fsdp"),
            P(None, "tensor"),
            P(None, "tensor"),
        ),
        check_vma=False,
    )
```

```python
import jax
import jax.numpy as jnp
from jax import lax
from jax.experimental import pallas as pl
from jax.experimental.pallas import tpu as pltpu
from jax.sharding import PartitionSpec as P


D = 768
HEADS = 12
BUCKETS = 32
BLOCK = 128
GBLOCK = 16
SLOTS = 64
ROWS = 256
FAR = 32
EXT = ROWS + 2 * BLOCK
ALL = EXT + 4 * FAR
KEYS = 3 * BLOCK + 4 * FAR
HALF = D // 2
FFS = 512
WIDE = 3 * FFS + D

f32 = jnp.float32
bf16 = jnp.bfloat16
tiny_eps = 1e-06
masked_score = -1e30


def dot(a, b):
    return lax.dot_general(a, b, (((1,), (0,)), ((), ())), preferred_element_type=f32)


def dot_nt(a, b):
    return lax.dot_general(a, b, (((1,), (1,)), ((), ())), preferred_element_type=f32)


def dot_tn(a, b):
    return lax.dot_general(a, b, (((0,), (0,)), ((), ())), preferred_element_type=f32)


def whole_spec(shape):
    return pl.BlockSpec(shape, lambda i: (0,) * len(shape))


def slab_spec(shape):
    return pl.BlockSpec((1,) + shape, lambda i: (i,) + (0,) * len(shape))


def shape_of(shape, dtype):
    return jax.ShapeDtypeStruct(shape, dtype)


def rsqrt_mean(v):
    return lax.rsqrt(jnp.mean(v * v, axis=-1, keepdims=True) + tiny_eps)


def row_term(v, r, gain, e):
    eg = e * gain
    return r * eg - v * (r * r * r) * jnp.mean(eg * v, axis=-1, keepdims=True)


def eye(rows, cols):
    at = lax.broadcasted_iota(jnp.int32, (rows, cols), 0)
    return (at == lax.broadcasted_iota(jnp.int32, (rows, cols), 1)).astype(bf16)


def pack_kernel(wq, wk, wv, wo, gate, up, down_t, out):
    rows = wq.shape[0]
    out_t = dot_nt(eye(rows, rows), wo[...]).astype(bf16)
    out[:, 0:FFS] = gate[...]
    out[:, FFS : 2 * FFS] = up[...]
    out[:, 2 * FFS : 3 * FFS] = down_t[...]
    at = 3 * FFS
    out[:, at : at + 128] = wq[:, 0:128]
    out[:, at + 128 : at + 256] = wk[:, 0:128]
    out[:, at + 256 : at + 384] = wv[:, 0:128]
    out[:, at + 384 : at + 512] = jnp.concatenate([wq[:, 128:192], wv[:, 128:192]], axis=1)
    out[:, at + 512 : at + 640] = jnp.concatenate([wk[:, 128:192], out_t[:, 128:192]], axis=1)
    out[:, at + 640 : at + 768] = out_t[:, 0:128]


def pack(*shards):
    return pl.pallas_call(
        pack_kernel, out_shape=shape_of((shards[0].shape[0], WIDE), bf16), name="pack"
    )(*shards)


def prep_kernel(tok, grad, order, gains, mem, tables, x, tokp, gop, pooled_ref, far):
    turn = order[...]
    v = dot(tok[...], turn)
    x[...] = (v * rsqrt_mean(v) * gains[0:1]).astype(bf16)
    tokp[...] = v.astype(bf16)
    gop[...] = dot(grad[...], turn).astype(bf16)
    pooled = dot(mem[...], x[...])
    pooled_ref[...] = pooled
    rows = (pooled * rsqrt_mean(pooled) * gains[2:3]).astype(bf16)
    at = lax.broadcasted_iota(jnp.int32, rows.shape, 0)
    far[...] = jnp.where(at == FAR - 1, jnp.broadcast_to(tables[...], rows.shape), rows)


def prep(*args):
    return pl.pallas_call(
        prep_kernel,
        out_shape=[
            shape_of((ROWS, D), bf16),
            shape_of((ROWS, D), bf16),
            shape_of((ROWS, D), bf16),
            shape_of((FAR, D), f32),
            shape_of((FAR, D), bf16),
        ],
        name="prep",
    )(*args)


def edge_kernel(left, right, order, gains, edge):
    for n, ref in enumerate((left, right)):
        v = dot(ref[...], order[...])
        edge[n * BLOCK : n * BLOCK + BLOCK] = (v * rsqrt_mean(v) * gains[0:1]).astype(bf16)


def edge_rows(*args):
    return pl.pallas_call(edge_kernel, out_shape=shape_of((2 * BLOCK, D), bf16), name="edge")(*args)


def join(w_s, pieces, step):
    for n in range(len(pieces) // 8):

        @pl.when(step == n)
        def _(n=n):
            def rows(i, carry):
                for k in range(8):
                    w_s[pl.ds(pl.multiple_of(k * 96 + i * 16, 16), 16), :] = pieces[8 * n + k][
                        pl.ds(pl.multiple_of(i * 16, 16), 16), :
                    ]
                return carry

            lax.fori_loop(0, 6, rows, 0)


attn_spec = pl.BlockSpec((96, D), lambda i: (0, 2))
ff_specs = [pl.BlockSpec((96, 3 * FFS), lambda i: (0, 0))] * 16


def keys_of(tile, c):
    return jnp.concatenate([tile[c * BLOCK : c * BLOCK + 3 * BLOCK], tile[EXT:ALL]], axis=0)


def fill_x(x_s, x, fars):
    own, edge = x
    x_s[0:BLOCK] = edge[0:BLOCK]
    x_s[BLOCK : BLOCK + ROWS] = own[...]
    x_s[BLOCK + ROWS : EXT] = edge[BLOCK:]
    for n, ref in enumerate(fars):
        x_s[EXT + n * FAR : EXT + n * FAR + FAR] = ref[...]


def turned(value, back):
    at = lax.broadcasted_iota(jnp.int32, value.shape, 0)
    size = value.shape[1]
    for bit in range(7):
        step = 1 << bit
        moved = pltpu.roll(value, size - step if back else step, 1)
        value = jnp.where((at >> bit) & 1 == 1, moved, value)
    return value


def attn_fwd_kernel(base, last, *refs):
    x, f0, f1, f2, f3 = (refs[:2],) + refs[2:6]
    pieces = refs[6:22]
    near_at, far_at, tables, mask = refs[22:26]
    refs = refs[26:]
    if last:
        before, tok, gains = refs[:3]
        refs = refs[3:]
        res, nf, p_ref, r_ref, a_ref, acc, x_s, w_s = refs
    else:
        acc, p_ref, r_ref, a_ref, x_s, w_s = refs
    step = pl.program_id(0)

    @pl.when(step == 0)
    def _():
        fill_x(x_s, x, (f0, f1, f2, f3))

    join(w_s, pieces, step)
    r = dot(x_s[...], w_s[:, 0:640]).astype(bf16)
    r_ref[0] = r
    low = lax.broadcasted_iota(jnp.int32, (BLOCK, 128), 1) < 64
    zero = jnp.zeros((BLOCK, 128), bf16)
    near_index = near_at[...]
    far_index = far_at[...]
    parts = [[None] * 3, [None] * 3]
    for j in range(3):
        head = (base + step) * 3 + j
        diagonal = jnp.zeros((1, 3 * BLOCK), f32)
        slots = jnp.zeros((16, 128), f32)
        for n in range(BUCKETS):
            diagonal = jnp.where(near_index == n, tables[head, n], diagonal)
            slots = jnp.where(far_index == n, tables[HEADS + head, n], slots)
        near = turned(jnp.broadcast_to(diagonal, (BLOCK, 3 * BLOCK)), False)
        q_all = r[:, 0:128] if j < 2 else r[:, 384:512]
        k_all = r[:, 128:256] if j < 2 else r[:, 512:640]
        v_all = r[:, 256:384] if j < 2 else r[:, 384:512]
        for c in range(2):
            q = q_all[BLOCK + c * BLOCK : 2 * BLOCK + c * BLOCK]
            q = jnp.where(low, zero, q) if j == 1 else jnp.where(low, q, zero)
            far = jnp.broadcast_to(slots[c * 8 : c * 8 + 8][:, None], (8, GBLOCK, 128)).reshape(BLOCK, 128)
            s = dot_nt(q, keys_of(k_all, c)) + jnp.concatenate([near, far], axis=1) + mask[c]
            e = jnp.exp(s - jnp.max(s, axis=-1, keepdims=True))
            p = (e * (1.0 / jnp.sum(e, axis=-1, keepdims=True))).astype(bf16)
            p_ref[0, c * 3 + j] = p
            parts[c][j] = dot(p, keys_of(v_all, c))
    for c in range(2):
        a_ref[0, c * BLOCK : c * BLOCK + BLOCK] = jnp.concatenate(
            [jnp.where(low, 0.0, parts[c][2]), jnp.where(low, parts[c][0], parts[c][1])], axis=1
        ).astype(bf16)
    part = dot_nt(a_ref[0], w_s[:, 512:768])

    @pl.when(step == 0)
    def _():
        acc[...] = before[...] + part if last else part

    @pl.when(step > 0)
    def _():
        acc[...] += part

    if last:

        @pl.when(step == pl.num_programs(0) - 1)
        def _():
            v = tok[...].astype(f32) + acc[...]
            res[...] = v
            nf[...] = (v * rsqrt_mean(v) * gains[1:2]).astype(bf16)


x_specs = [whole_spec((ROWS, D)), whole_spec((2 * BLOCK, D))] + [whole_spec((FAR, D))] * 4


def attn_fwd(base, x, fars, pieces, near_at, far_at, tables, mask, *rest):
    last = len(rest) > 0
    outs = [
        (slab_spec((6, BLOCK, KEYS)), shape_of((2, 6, BLOCK, KEYS), bf16)),
        (slab_spec((ALL, 640)), shape_of((2, ALL, 640), bf16)),
        (slab_spec((ROWS, 256)), shape_of((2, ROWS, 256), bf16)),
    ]
    wide = (whole_spec((ROWS, D)), shape_of((ROWS, D), f32))
    if last:
        outs = [wide, (whole_spec((ROWS, D)), shape_of((ROWS, D), bf16))] + outs
    else:
        outs = [wide] + outs
    return pl.pallas_call(
        lambda *refs: attn_fwd_kernel(base, last, *refs),
        grid=(2,),
        in_specs=x_specs
        + [attn_spec] * 16
        + [
            whole_spec((1, 3 * BLOCK)),
            whole_spec((16, 128)),
            pl.BlockSpec(memory_space=pltpu.SMEM),
            whole_spec((2, BLOCK, KEYS)),
        ]
        + ([whole_spec((ROWS, D)), whole_spec((ROWS, D)), whole_spec((8, D))] if last else []),
        out_specs=[o[0] for o in outs],
        out_shape=[o[1] for o in outs],
        scratch_shapes=([pltpu.VMEM((ROWS, D), f32)] if last else [])
        + [pltpu.VMEM((ALL, D), bf16), pltpu.VMEM((D, D), bf16)],
        name="attn_fwd_b" if last else "attn_fwd_a",
    )(*x, *fars, *pieces, near_at, far_at, tables, mask, *rest)


def attn_bwd_kernel(slabs, more, last, *refs):
    x, f0, f1, f2, f3, rl = (refs[:2],) + refs[2:7]
    pieces = refs[7 : 7 + 8 * slabs]
    refs = refs[7 + 8 * slabs :]
    r_ref, p_ref, a_ref = refs[:3]
    refs = refs[3:]
    if more:
        before = refs[0]
        refs = refs[1:]
    if last:
        where_ref = refs[0]
        down, doth, near_ref, far_ref, own, fown, s1, s2, s3, s4, xg, x_s, w_s, dr_s = refs[1:]
    else:
        down, doth, near_ref, far_ref, xg, x_s, w_s, dr_s = refs
    step = pl.program_id(0)

    @pl.when(step == 0)
    def _():
        fill_x(x_s, x, (f0, f1, f2, f3))

    join(w_s, pieces, step)
    da = dot(rl[...], w_s[:, 512:768]).astype(bf16)
    low = lax.broadcasted_iota(jnp.int32, (BLOCK, 128), 1) < 64
    zero = jnp.zeros((BLOCK, 128), bf16)
    r = r_ref[0]
    dr_s[...] = jnp.zeros((ALL, 640), f32)

    def add_keys(n, c, value):
        lanes = slice(n * 128, n * 128 + 128)
        dr_s[c * BLOCK : c * BLOCK + 3 * BLOCK, lanes] += value[: 3 * BLOCK]
        dr_s[EXT:ALL, lanes] += value[3 * BLOCK :]

    near = [None, None, None]
    for c in range(2):
        rows = slice(BLOCK + c * BLOCK, 2 * BLOCK + c * BLOCK)
        held = None
        for j in range(3):
            p = p_ref[0, c * 3 + j]
            q = r[rows, 0:128] if j < 2 else r[rows, 384:512]
            q = jnp.where(low, zero, q) if j == 1 else jnp.where(low, q, zero)
            k = keys_of(r[:, 128:256] if j < 2 else r[:, 512:640], c)
            v = keys_of(r[:, 256:384] if j < 2 else r[:, 384:512], c)
            do = da[c * BLOCK : c * BLOCK + BLOCK, (128 if j < 2 else 0) : (256 if j < 2 else 128)]
            do = jnp.where(low, do, zero) if j == 0 else jnp.where(low, zero, do)
            wide = p.astype(f32)
            dp = dot_nt(do, v)
            ds = wide * (dp - jnp.sum(wide * dp, axis=-1, keepdims=True))
            near[j] = ds[:, : 3 * BLOCK] if c == 0 else near[j] + ds[:, : 3 * BLOCK]
            far_ref[0, j, c * 8 : c * 8 + 8] = jnp.sum(
                ds[:, 3 * BLOCK :].reshape(8, GBLOCK, 128), axis=1
            )
            dl = ds.astype(bf16)
            dq = dot(dl, k)
            add_keys(1 if j < 2 else 4, c, dot_tn(dl, q))
            add_keys(2 if j < 2 else 3, c, dot_tn(p, do))
            if j == 0:
                held = dq
            elif j == 1:
                dr_s[rows, 0:128] = jnp.where(low, held, dq)
            else:
                dr_s[rows, 384:512] += jnp.where(low, dq, 0.0)
    for j in range(3):
        near_ref[0, j : j + 1] = jnp.sum(turned(near[j], True), axis=0, keepdims=True)
    dr = dr_s[...].astype(bf16)
    part = dot_nt(dr, w_s[:, 0:640])

    @pl.when(step == 0)
    def _():
        xg[...] = before[...] + part if more else part

    @pl.when(step > 0)
    def _():
        xg[...] += part

    for ref, base in ((down, 0), (doth, HALF)):
        g = dot_tn(x_s[:, base : base + HALF], dr)
        go = dot_tn(rl[:, base : base + HALF], a_ref[0])
        ref[0, :, 0:512] = g[:, 0:512].astype(bf16)
        ref[0, :, 512:640] = (g[:, 512:640] + go[:, 0:128]).astype(bf16)
        ref[0, :, 640:768] = go[:, 128:256].astype(bf16)
    if last:

        @pl.when(step == pl.num_programs(0) - 1)
        def _():
            own[...] = xg[BLOCK : BLOCK + ROWS]
            fown[...] = xg[EXT : EXT + FAR]
            lo = xg[0:BLOCK].astype(bf16)
            hi = xg[BLOCK + ROWS : EXT].astype(bf16)
            odd = where_ref[0] > 0
            s1[0:BLOCK] = jnp.where(odd, lo, hi)
            s4[...] = jnp.where(odd, hi, lo)
            s1[BLOCK:] = xg[EXT + FAR : EXT + 2 * FAR].astype(bf16)
            s2[...] = xg[EXT + 2 * FAR : EXT + 3 * FAR].astype(bf16)
            s3[...] = xg[EXT + 3 * FAR : EXT + 4 * FAR].astype(bf16)


def attn_bwd(x, fars, rl, pieces, offset, r, p, a, *rest):
    slabs = len(pieces) // 8
    more = len(rest) > 0
    last = len(rest) > 1

    def part_spec(shape):
        return pl.BlockSpec((1,) + shape, lambda i: (i + offset,) + (0,) * len(shape))

    outs = [
        (slab_spec((HALF, D)), shape_of((slabs, HALF, D), bf16)),
        (slab_spec((HALF, D)), shape_of((slabs, HALF, D), bf16)),
        (slab_spec((3, 3 * BLOCK)), shape_of((slabs, 3, 3 * BLOCK), f32)),
        (slab_spec((3, 16, 128)), shape_of((slabs, 3, 16, 128), f32)),
    ]
    if last:
        for rows, dtype in (
            (ROWS, f32), (FAR, f32), (BLOCK + FAR, bf16), (FAR, bf16), (FAR, bf16), (BLOCK, bf16),
        ):
            outs.append((whole_spec((rows, D)), shape_of((rows, D), dtype)))
    else:
        outs.append((whole_spec((ALL, D)), shape_of((ALL, D), f32)))
    return pl.pallas_call(
        lambda *refs: attn_bwd_kernel(slabs, more, last, *refs),
        grid=(slabs,),
        in_specs=x_specs
        + [whole_spec((ROWS, D))]
        + [attn_spec] * (8 * slabs)
        + [part_spec((ALL, 640)), part_spec((6, BLOCK, KEYS)), part_spec((ROWS, 256))]
        + ([whole_spec((ALL, D))] if more else [])
        + ([pl.BlockSpec(memory_space=pltpu.SMEM)] if last else []),
        out_specs=[o[0] for o in outs],
        out_shape=[o[1] for o in outs],
        scratch_shapes=([pltpu.VMEM((ALL, D), f32)] if last else [])
        + [pltpu.VMEM((ALL, D), bf16), pltpu.VMEM((D, D), bf16), pltpu.VMEM((ALL, 640), f32)],
    )(*x, *fars, rl, *pieces, r, p, a, *rest)


def ff_kernel(last, *refs):
    nf, go = refs[:2]
    pieces = refs[2:18]
    refs = refs[18:]
    if last:
        out_a, ng_a, res, gains, order = refs[:5]
        down, doth, output, res_grad, rl, gain_grad, out_acc, ng_acc, w_s = refs[5:]
    else:
        down, doth, out_acc, ng_acc, w_s = refs
    step = pl.program_id(0)
    join(w_s, pieces, step)
    gate = dot(nf[...], w_s[:, 0:FFS])
    up = dot(nf[...], w_s[:, FFS : 2 * FFS])
    hg = dot(go[...], w_s[:, 2 * FFS : 3 * FFS])
    root = 0.7978845608028654
    t = jnp.tanh(root * (gate + 0.044715 * gate * gate * gate))
    cdf = 0.5 * (1.0 + t)
    act = gate * cdf
    slope = cdf + 0.5 * gate * (1.0 - t * t) * (root * (1.0 + 3.0 * 0.044715 * gate * gate))
    hidden = (act * up).astype(bf16)
    both = jnp.concatenate([(hg * up * slope).astype(bf16), (hg * act).astype(bf16)], axis=1)
    out = dot_nt(hidden, w_s[:, 2 * FFS : 3 * FFS])
    ng = dot_nt(both, w_s[:, 0 : 2 * FFS])

    @pl.when(step == 0)
    def _():
        out_acc[...] = out_a[...] + out if last else out
        ng_acc[...] = ng_a[...] + ng if last else ng

    @pl.when(step > 0)
    def _():
        out_acc[...] += out
        ng_acc[...] += ng

    for ref, base in ((down, 0), (doth, HALF)):
        ref[0, :, 0 : 2 * FFS] = dot_tn(nf[:, base : base + HALF], both).astype(bf16)
        ref[0, :, 2 * FFS : 3 * FFS] = dot_tn(go[:, base : base + HALF], hidden).astype(bf16)
    if last:

        @pl.when(step == pl.num_programs(0) - 1)
        def _():
            v = res[...]
            r = rsqrt_mean(v)
            e = ng_acc[...]
            output[...] = dot_nt((v + out_acc[...]).astype(bf16), order[...]).astype(bf16)
            total = go[...].astype(f32) + row_term(v, r, gains[1:2], e)
            res_grad[...] = total
            rl[...] = total.astype(bf16)
            gain_grad[...] = jnp.sum(e * v * r, axis=0, keepdims=True)


def ff_both(nf, go, pieces, *rest):
    last = len(rest) > 0
    wide = (whole_spec((ROWS, D)), shape_of((ROWS, D), f32))
    narrow = (whole_spec((ROWS, D)), shape_of((ROWS, D), bf16))
    outs = [(slab_spec((HALF, 3 * FFS)), shape_of((2, HALF, 3 * FFS), bf16))] * 2
    if last:
        outs = outs + [narrow, wide, narrow, (whole_spec((1, D)), shape_of((1, D), f32))]
    else:
        outs = outs + [wide, wide]
    return pl.pallas_call(
        lambda *refs: ff_kernel(last, *refs),
        grid=(2,),
        in_specs=[whole_spec((ROWS, D))] * 2
        + ff_specs
        + ([whole_spec((ROWS, D))] * 3 + [whole_spec((8, D)), whole_spec((D, D))] if last else []),
        out_specs=[o[0] for o in outs],
        out_shape=[o[1] for o in outs],
        scratch_shapes=([pltpu.VMEM((ROWS, D), f32)] * 2 if last else []) + [pltpu.VMEM((D, 3 * FFS), bf16)],
        name="ff_a" if last else "ff_b",
    )(nf, go, *pieces, *rest)


def split3(value):
    parts = []
    for _ in range(3):
        parts.append(value.astype(bf16))
        value = value - parts[-1].astype(f32)
    return parts


def post_kernel(
    where_ref, own, f0, r1, r2, r3, r4, res_grad, tok, pooled, mem, gains, order, gain_ff,
    near_0, near_1, near_b, far_0, far_1, far_b, near_at, far_at, grad, small,
):
    e = f0[...] + r1[BLOCK:].astype(f32) + r2[...].astype(f32) + r3[...].astype(f32)
    v = pooled[...]
    r = rsqrt_mean(v)
    spread = row_term(v, r, gains[2:3], e)
    gain_global = jnp.sum(e * v * r, axis=0, keepdims=True)
    odd = where_ref[0] > 0
    near = r1[0:BLOCK].astype(f32)
    other = jnp.where(where_ref[1] > 0, r4[...].astype(f32), 0.0)
    wide = own[...] + jnp.concatenate(
        [jnp.where(odd, near, other), jnp.where(odd, other, near)], axis=0
    )
    for part in split3(spread):
        wide = wide + dot_tn(mem[...], part)
    v = tok[...].astype(f32)
    r = rsqrt_mean(v)
    rest = res_grad[...] + row_term(v, r, gains[0:1], wide)
    sums = jnp.concatenate(
        [jnp.sum(wide * v * r, axis=0, keepdims=True), gain_ff[...], gain_global, jnp.zeros((5, D), f32)]
    )
    total = jnp.zeros((ROWS, D), f32)
    gain_sums = jnp.zeros((8, D), f32)
    for part, gain_part in zip(split3(rest), split3(sums)):
        total = total + dot_nt(part, order[...])
        gain_sums = gain_sums + dot_nt(gain_part, order[...])
    grad[...] = total
    small[0:8] = gain_sums
    bucket = lax.broadcasted_iota(jnp.int32, (BUCKETS, 3 * BLOCK), 0)
    near_hot = (jnp.broadcast_to(near_at[...], bucket.shape) == bucket).astype(bf16)
    far_hot = [
        (jnp.broadcast_to(far_at[a : a + 1], (BUCKETS, 128)) == bucket[:, 0:128]).astype(bf16) for a in range(16)
    ]
    near_grad = jnp.concatenate([near_0[0], near_1[0], near_b[0], near_b[1]], axis=0)
    far_of = [far_0.at[0], far_1.at[0], far_b.at[0], far_b.at[1]]
    near_table = sum(dot_nt(part, near_hot) for part in split3(near_grad))
    far_table = jnp.zeros((HEADS, BUCKETS), f32)
    for a in range(16):
        far_grad = jnp.concatenate([ref[:, a] for ref in far_of], axis=0)
        far_table = far_table + sum(dot_nt(part, far_hot[a]) for part in split3(far_grad))
    at = lax.broadcasted_iota(jnp.int32, (16, HEADS), 0)
    col = lax.broadcasted_iota(jnp.int32, (16, HEADS), 1)
    place = jnp.zeros((16, HEADS), f32)
    for k in range(4):
        place = jnp.where((col // 3 == k) & (at == col % 3 + 3 * (where_ref[2] ^ k)), 1.0, place)
    place = place.astype(bf16)
    near_sum = sum(dot(place, part) for part in split3(near_table))
    far_sum = sum(dot(place, part) for part in split3(far_table))
    small[8:24] = jnp.zeros((16, D), f32)
    small[8:24, 0:BUCKETS] = near_sum
    small[8:24, 128 : 128 + BUCKETS] = far_sum


def post(*args):
    in_vmem = pl.BlockSpec(memory_space=pltpu.VMEM)
    return pl.pallas_call(
        post_kernel,
        in_specs=[pl.BlockSpec(memory_space=pltpu.SMEM)] + [in_vmem] * (len(args) - 1),
        out_shape=[shape_of((ROWS, D), f32), shape_of((24, D), f32)],
        name="post",
    )(*args)


def unpack_kernel(s0, s1, s2, s3, q, k, v, o):
    wide = s0[...].astype(f32) + s1[...].astype(f32) + s2[...].astype(f32) + s3[...].astype(f32)
    q[:, 0:128] = wide[:, 0:128]
    k[:, 0:128] = wide[:, 128:256]
    v[:, 0:128] = wide[:, 256:384]
    q[:, 128:192] = wide[:, 384:448]
    v[:, 128:192] = wide[:, 448:512]
    k[:, 128:192] = wide[:, 512:576]
    out = jnp.concatenate([wide[:, 640:768], wide[:, 576:640]], axis=1)
    o[...] = out.T if o.shape[0] == 192 else out


def unpack(*slabs):
    rows = slabs[0].shape[0]
    turn = rows % 32 == 0
    q, k, v, o = pl.pallas_call(
        unpack_kernel,
        out_shape=[shape_of((rows, 192), f32)] * 3 + [shape_of((192, rows) if turn else (rows, 192), f32)],
        name="unpack",
    )(*slabs)
    return q, k, v, o if turn else o.T


def swap(x, axis, mask):
    size = lax.axis_size(axis)
    return lax.ppermute(x, axis, [(i, i ^ mask) for i in range(size)])


def high_bits():
    return list(range(3, lax.axis_size("fsdp").bit_length() - 1))


def near_swaps(x):
    got = [x]
    for n in (1, 2, 3):
        got.append(swap(x, "fsdp", n << 1))
    return got


def gather_high(shard):
    for bit in high_bits():
        shard = jnp.concatenate([shard, swap(shard, "fsdp", 1 << bit)], axis=0)
    return shard


def gather_tensor(x):
    got = []
    for k in (1, 2, 3):
        got.append(swap(x, "tensor", k))
    return got


def scatter_pair(sources, behind=None):
    dtype = sources[0][0].dtype
    came = []
    for _, oth in sources:
        came.append(swap(oth, "fsdp", 1))

    def piece(n):
        rows = slice(n * 96, n * 96 + 96)
        return jnp.concatenate(
            [own[:, rows].astype(f32) + got[:, rows].astype(f32) for (own, _), got in zip(sources, came)]
        )

    total = piece(0)
    sends = [piece(n).astype(dtype) for n in (1, 2, 3)]
    came = []
    for n in (1, 2, 3):
        came.append(swap(sends[n - 1], "fsdp", n << 1))
    if behind is not None:
        came, _ = lax.optimization_barrier((came, behind))
    total = total + came[0].astype(f32) + came[1].astype(f32) + came[2].astype(f32)
    total = total.astype(dtype)
    for bit in high_bits()[::-1]:
        half = total.shape[1] // 2
        total = total[:, :half] + swap(total[:, half:], "fsdp", 1 << bit)
    return total, sends


def scatter_tensor(slabs):
    got = [slabs[0]]
    for k in (1, 2, 3):
        got.append(swap(slabs[k], "tensor", k))
    return got


def inner(
    tokens, ln_attn, ln_ff, ln_global, w_query, w_key, w_value, w_out, wi_gate, wi_up, wo_ff,
    table_local, table_global, local_onehot, global_onehot, segment, grad_out,
):
    count = lax.axis_size("fsdp")
    width = D // count
    f = lax.axis_index("fsdp")
    z = lax.axis_index("tensor")
    last = lax.axis_size("tensor") - 1
    up_one = [(i, i + 1) for i in range(last)]
    down_one = [(i + 1, i) for i in range(last)]

    gains = jnp.stack([ln_attn, ln_ff, ln_global])[:, None, :]
    for bit in high_bits():
        gains = jnp.concatenate([gains, swap(gains, "fsdp", 1 << bit)], axis=1)
    gains = jnp.concatenate(near_swaps(gains), axis=1)
    gains = jnp.concatenate([gains, swap(gains, "fsdp", 1)], axis=1)
    gains = jnp.pad(gains.reshape(3, D).astype(f32), ((0, 5), (0, 0)))
    left = lax.ppermute(tokens[ROWS - BLOCK :], "tensor", up_one)
    right = lax.ppermute(tokens[:BLOCK], "tensor", down_one)

    shard = gather_high(pack(w_query, w_key, w_value, w_out, wi_gate, wi_up, wo_ff.T))
    slabs = [shard] + gather_tensor(shard)
    tables = jnp.concatenate([table_local.T.reshape(1, -1), table_global.T.reshape(1, -1)], axis=1)
    tables = jnp.pad(tables, ((0, 0), (0, D - tables.shape[1])))

    seg_row, near_hot, tables, gains, f_late = lax.optimization_barrier(
        (segment[0], local_onehot[0], tables, gains, f)
    )

    true_at = jnp.arange(D, dtype=jnp.int32)
    piece = true_at // 96
    high = (true_at % 96) // width
    relative = (piece // 4) | ((piece & 3) << 1) | (high << 3)
    source = (f_late ^ relative) * width + true_at % width
    order = (true_at[:, None] == source[None, :]).astype(bf16)

    parts = seg_row.reshape(4, ROWS)
    rel = jnp.arange(4, dtype=jnp.int32) ^ z
    seg_rel = jnp.take(parts, rel, axis=0)
    here = jnp.arange(ROWS, dtype=jnp.int32)
    starts = (here % GBLOCK == 0)[None] | (
        seg_rel != jnp.concatenate([seg_rel[:, :1], seg_rel[:, :-1]], axis=1)
    )
    triangle = (here[:, None] <= here[None, :]).astype(bf16)
    piece_rel = dot(starts.astype(bf16), triangle).astype(jnp.int32) - 1
    member = (piece_rel[0] == jnp.arange(FAR, dtype=jnp.int32)[:, None]).astype(bf16)
    own_hot = lax.dynamic_slice(global_onehot, (z * 16, 0, 0), (16, SLOTS, BUCKETS))
    is_in = piece_rel[:, None, :] == jnp.arange(FAR, dtype=jnp.int32)[:, None]
    slot_rel = rel[:, None] * (ROWS // GBLOCK) + here[None] // GBLOCK
    piece_doc = jnp.max(jnp.where(is_in, seg_rel[:, None, :], -1), axis=2).reshape(4 * FAR)
    piece_slot = jnp.max(jnp.where(is_in, slot_rel[:, None, :], -1), axis=2).reshape(4 * FAR)

    x_own, tok, go, pooled, far_rows = prep(tokens, grad_out, order, gains, member, tables)
    x = (x_own, edge_rows(left, right, order, gains))
    fars = [far_rows] + gather_tensor(far_rows)

    tables = jnp.stack([far[FAR - 1, : 6 * BUCKETS] for far in fars])
    tables = tables.reshape(4, 2, 3, BUCKETS).transpose(1, 0, 2, 3).reshape(2 * HEADS, BUCKETS).astype(f32)

    padded = jnp.concatenate([jnp.full((BLOCK,), -1, jnp.int32), seg_row, jnp.full((BLOCK,), -1, jnp.int32)])
    seg_ext = lax.dynamic_slice(padded, (z * ROWS,), (EXT,))
    seg_own = seg_ext[BLOCK : BLOCK + ROWS].reshape(2, BLOCK)
    seg_keys = jnp.stack([seg_ext[: 3 * BLOCK], seg_ext[BLOCK:]])
    offset = jnp.arange(3 * BLOCK, dtype=jnp.int32)[None] - BLOCK - jnp.arange(BLOCK, dtype=jnp.int32)[:, None]
    near_ok = (jnp.abs(offset) < BLOCK)[None] & (seg_own[:, :, None] == seg_keys[:, None, :])
    far_ok = seg_own[:, :, None] == piece_doc[None, None, :]
    mask = jnp.where(jnp.concatenate([near_ok, far_ok], axis=2), 0.0, masked_score).astype(f32)
    bucket = jnp.arange(BUCKETS, dtype=jnp.int32)
    near_at = jnp.sum(near_hot * bucket, axis=1)[None]
    slot_at = jnp.sum(own_hot * bucket, axis=2)
    slot_is = piece_slot[None, :] == jnp.arange(SLOTS, dtype=jnp.int32)[:, None]
    far_at = dot(slot_at.astype(bf16), slot_is.astype(bf16)).astype(jnp.int32)

    small_work = (mask, near_at, far_at, tables)
    whole = []
    for n, slab in enumerate(slabs):
        own_pieces = near_swaps(slab)
        if n == 1:
            own_pieces, (mask, near_at, far_at, tables) = lax.optimization_barrier((own_pieces, small_work))
        whole.append(own_pieces + [swap(piece, "fsdp", 1) for piece in own_pieces])
    pair_a = whole[0] + whole[1]
    pair_b = whole[2] + whole[3]

    acc, p_a, r_a, at_a = attn_fwd(0, x, fars, pair_a, near_at, far_at, tables, mask)
    residual, nf, p_b, r_b, at_b = attn_fwd(
        2, x, fars, pair_b, near_at, far_at, tables, mask, acc, tok, gains
    )
    fo_b, ft_b, out_b, ng_b = ff_both(nf, go, pair_b)
    fo_a, ft_a, output, res_grad, rl, gain_ff = ff_both(
        nf, go, pair_a, out_b, ng_b, residual, gains, order
    )
    sum_fb, _ = scatter_pair([(fo_b, ft_b)])
    sum_fa, _ = scatter_pair([(fo_a, ft_a)])
    where = jnp.stack([z & 1, ((z == 1) | (z == 2)).astype(jnp.int32), z]).astype(jnp.int32)
    do_b, dt_b, nb_b, fb_b, xg = attn_bwd(x, fars, rl, pair_b, 0, r_b, p_b, at_b)
    do_1, dt_1, nb_1, fb_1, xg = attn_bwd(x, fars, rl, whole[1], 1, r_a, p_a, at_a, xg)
    do_0, dt_0, nb_0, fb_0, own, f0, s1, s2, s3, s4 = attn_bwd(
        x, fars, rl, whole[0], 0, r_a, p_a, at_a, xg, where
    )
    sum_aa, sends = scatter_pair([(do_0, dt_0), (do_1, dt_1)])
    sum_ab, _ = scatter_pair([(do_b, dt_b)], sends)
    got = []
    for k, sent in ((1, s1), (2, s2), (3, s3)):
        got.append(swap(sent, "tensor", k))
    got.append(lax.ppermute(s4, "tensor", [(1, 2), (2, 1)]))
    grad_tokens, small = post(
        where, own, f0, *got, res_grad, tok, pooled, member, gains, order, gain_ff,
        nb_0, nb_1, nb_b, fb_0, fb_1, fb_b, near_at, far_at,
    )
    got = [small] + gather_tensor(small)
    got, _ = lax.optimization_barrier((got, sum_aa))
    small = (got[0] + got[1]) + (got[2] + got[3])
    small = small + swap(small, "fsdp", 1)
    got = near_swaps(small)
    small = (got[0] + got[1]) + (got[2] + got[3])
    for bit in high_bits():
        small = small + swap(small, "fsdp", 1 << bit)
    gain_sum = lax.dynamic_slice(small, (0, f * width), (3, width))
    table_sum = lax.dynamic_slice(small, (8 + 3 * z, 0), (3, 256))

    parts = scatter_tensor([sum_fa[0], sum_fa[1], sum_fb[0], sum_fb[1]])
    ff_sum = sum(part.astype(f32) for part in parts)
    last_sums = scatter_tensor([sum_aa[0], sum_aa[1], sum_ab[0], sum_ab[1]])
    grad_query, grad_key, grad_value, grad_w_out = unpack(*last_sums)
    return (
        output,
        grad_tokens,
        gain_sum[0],
        gain_sum[1],
        gain_sum[2],
        grad_query,
        grad_key,
        grad_value,
        grad_w_out,
        ff_sum[:, 0:FFS],
        ff_sum[:, FFS : 2 * FFS],
        ff_sum[:, 2 * FFS : 3 * FFS].T,
        table_sum[:, 0:BUCKETS].T,
        table_sum[:, 128 : 128 + BUCKETS].T,
    )


def solution(mesh):
    return jax.shard_map(
        inner,
        mesh=mesh,
        in_specs=(
            P(("fsdp", "tensor"), None),
            P("fsdp"),
            P("fsdp"),
            P("fsdp"),
            P("fsdp", "tensor"),
            P("fsdp", "tensor"),
            P("fsdp", "tensor"),
            P("tensor", "fsdp"),
            P("fsdp", "tensor"),
            P("fsdp", "tensor"),
            P("tensor", "fsdp"),
            P(None, "tensor"),
            P(None, "tensor"),
            P(),
            P(),
            P("fsdp", None),
            P(("fsdp", "tensor"), None),
        ),
        out_specs=(
            P(("fsdp", "tensor"), None),
            P(("fsdp", "tensor"), None),
            P("fsdp"),
            P("fsdp"),
            P("fsdp"),
            P("fsdp", "tensor"),
            P("fsdp", "tensor"),
            P("fsdp", "tensor"),
            P("tensor", "fsdp"),
            P("fsdp", "tensor"),
            P("fsdp", "tensor"),
            P("tensor", "fsdp"),
            P(None, "tensor"),
            P(None, "tensor"),
        ),
        check_vma=False,
    )
```
